32 devices in a mesh: section: 2 (over core), stream: 4 (over y, x), slab: 4 (over z).
Axes of the slice: x: 2, y: 2, z: 4, core: 2. Of those that a mesh axis runs over, the one named last changes fastest.
Arguments:
- state: float32 [2, 4, 256, 64, 128], P('section', None, 'stream', 'slab'), may hold values from -6 to 6
- source_mask: int32 [16, 4], P(None, 'slab'), may hold values 0 or 1
- deriv_x: float32 [256, 256], replicated, may hold values from -0.28125 to 0.28125
- deriv_z: float32 [128, 128], replicated, may hold values from -0.397747564 to 0.397747564
- filter_x: float32 [256, 256], replicated, may hold values from -0.375 to 0.375
- filter_z: float32 [128, 128], replicated, may hold values from -0.5 to 0.5
Outputs:
- advanced: float32 [2, 4, 256, 64, 128], P('section', None, 'stream', 'slab')
The draws below stay inside these ranges and needn't reach their ends.
All inputs are finite; a program needn't handle non-finite values. No bound on the sum of `source_mask` on one device may be relied on, other than what follows from the above.
Results may differ from the reference program's by a relative error of at most 0.0001.
Values sent between devices are 32-bit elements; how exact they have to be, the bound alone decides.
A program may use at most 128 MiB of HBM per device.

```python
import math
import jax
import jax.numpy as jnp
from jax import lax

NX = 256
NZ = 128
SEGMENTS = 8
MBLK = 16
NY = 64


def dense_operator(key, order):
    limit = 4.5 / math.sqrt(order)
    values = jnp.clip(3.0 / math.sqrt(order) * jax.random.normal(key, (order, order), jnp.float32), -limit, limit)
    return values


def draw_deriv_x(key, part):
    return dense_operator(jax.random.fold_in(key, 11), NX)


def draw_deriv_z(key, part):
    return dense_operator(jax.random.fold_in(key, 23), NZ)


def touch_ends(array, stream_key, low, largest):
    dims = array.shape
    place = [jax.random.randint(jax.random.fold_in(stream_key, axis), (), 0, dims[axis]) for axis in range(len(dims))]
    array = array.at[tuple(place)].set(low)
    longest = dims.index(max(dims))
    place[longest] = (place[longest] + 1) % dims[longest]
    return array.at[tuple(place)].set(largest)


def shard_levels(own_key, dims, cuts, least, largest):
    def one(position, blocks):
        steps = jax.random.uniform(jax.random.fold_in(jax.random.fold_in(own_key, 6), position), (blocks,), jnp.float32, least / len(cuts), largest / len(cuts))
        return jnp.repeat(jnp.exp(steps), dims[position] // blocks).reshape((-1,) + (1,) * (len(dims) - position - 1))

    level = one(*cuts[0])
    for cut in cuts[1:]:
        level = level * one(*cut)
    return level


def normal_values(own_key, dims, width, bound, cuts=(), held_as=jnp.bfloat16):
    entries = width * jax.random.normal(own_key, dims, jnp.float32)
    if cuts:
        entries = entries * shard_levels(own_key, dims, cuts, -0.22, 0.18)
    return jnp.clip(entries, -bound, bound).astype(held_as)


def setup_inputs(seed: int = 0) -> dict:
    arg_keys = jax.random.split(jax.random.key(seed), 7)
    return {
        "state": normal_values(arg_keys[0], (2, 4, NX, NY, NZ), 1.0, 6.0, ((0, 2), (2, 4), (3, 4)), jnp.float32),
        "source_mask": touch_ends((jax.random.randint(arg_keys[1], (NX // MBLK, NY // MBLK), 0, 2) < 1).astype(jnp.int32), jax.random.fold_in(arg_keys[1], 1), 0, 1),
        "deriv_x": draw_deriv_x(jax.random.fold_in(arg_keys[6], 71), 0),
        "deriv_z": draw_deriv_z(jax.random.fold_in(arg_keys[6], 71), 0),
        "filter_x": normal_values(arg_keys[4], (NX, NX), NX ** -0.5, 0.375, (), jnp.float32),
        "filter_z": normal_values(arg_keys[5], (NZ, NZ), NZ ** -0.5, 0.5, (), jnp.float32),
    }


mach_number = 0.5
time_step = 0.05
filter_weight = 0.25


def central_slope(values, which_dim):
    widths = [(0, 0), (0, 0), (0, 0)]
    widths[which_dim] = (1, 1)
    padded = jnp.pad(values, widths)
    length = values.shape[which_dim]
    upper_side = lax.slice_in_dim(padded, 2, length + 2, axis=which_dim)
    lower_side = lax.slice_in_dim(padded, 0, length, axis=which_dim)
    return 0.5 * (upper_side - lower_side)


def lamb_vector(velocity):
    speed_x, speed_y, speed_z = velocity[0], velocity[1], velocity[2]
    vortex_x = central_slope(speed_z, 1) - central_slope(speed_y, 2)
    vortex_y = central_slope(speed_x, 2) - central_slope(speed_z, 0)
    vortex_z = central_slope(speed_y, 0) - central_slope(speed_x, 1)
    return jnp.stack([vortex_y * speed_z - vortex_z * speed_y,
                      vortex_z * speed_x - vortex_x * speed_z,
                      vortex_x * speed_y - vortex_y * speed_x])


def along_x(matrix, fields):
    return jnp.einsum("ij,fjyz->fiyz", matrix, fields, precision=lax.Precision.HIGHEST)


def along_z(matrix, fields):
    return jnp.einsum("fxyz,kz->fxyk", fields, matrix, precision=lax.Precision.HIGHEST)


def fourth_slope_y(fields):
    padded = jnp.pad(fields, ((0, 0), (0, 0), (2, 2), (0, 0)))
    length = fields.shape[2]

    def shifted(offset):
        return lax.slice_in_dim(padded, 2 + offset, 2 + offset + length, axis=2)

    return (8.0 * (shifted(1) - shifted(-1)) - (shifted(2) - shifted(-2))) / 12.0


def tendency(fields, slope_x, slope_y, slope_z, forcing):
    press_rate = -mach_number * slope_x[0] - slope_x[1] - slope_y[1] - slope_z[1]
    axial_rate = -mach_number * slope_x[1] - slope_x[0] + forcing[0]
    normal_rate = -mach_number * slope_x[2] - slope_y[0] + forcing[1]
    third_rate = -mach_number * slope_x[3] - slope_z[0] + forcing[2]
    return jnp.stack([press_rate, axial_rate, normal_rate, third_rate])


def substep(fields, forcing, deriv_x, deriv_z):
    slope_x = along_x(deriv_x, fields)
    slope_y = fourth_slope_y(jnp.stack([fields[0], fields[2]]))
    slope_z = along_z(deriv_z, jnp.stack([fields[0], fields[3]]))
    return fields + time_step * tendency(fields, slope_x, slope_y, slope_z, forcing)


def reference(state, source_mask, deriv_x, deriv_z, filter_x, filter_z):
    region = jnp.repeat(jnp.repeat(source_mask, MBLK, axis=0), MBLK, axis=1).astype(jnp.float32)
    flow_now = state[0]
    sound_now = state[1]
    no_forcing = jnp.zeros((3,) + flow_now.shape[1:], jnp.float32)
    forcing = no_forcing
    for segment_index in range(SEGMENTS):
        if segment_index % 2 == 0:
            forcing = -region[None, :, :, None] * lamb_vector(flow_now[1:4])
        flow_now = substep(flow_now, no_forcing, deriv_x, deriv_z)
        sound_now = substep(sound_now, forcing, deriv_x, deriv_z)

    def smooth(fields):
        return fields + filter_weight * along_x(filter_x, fields) + filter_weight * along_z(filter_z, fields)

    return jnp.stack([smooth(flow_now), smooth(sound_now)])
```

```python
import functools
import math

import jax
import jax.numpy as jnp
from jax import lax
from jax.experimental import pallas as pl
from jax.experimental.pallas import tpu as pltpu
from jax.sharding import PartitionSpec as P

SEGMENTS = 8
MBLK = 16

mach_number = 0.5
time_step = 0.05
filter_weight = 0.25


def split_parts(value):
    high = value.astype(jnp.bfloat16)
    low = (value - high.astype(jnp.float32)).astype(jnp.bfloat16)
    return high, low


def dot_parts(left, right):
    dot = functools.partial(jnp.dot, preferred_element_type=jnp.float32)
    return dot(left[0], right[0]) + (dot(left[0], right[1]) + dot(left[1], right[0]))


def wide(ref):
    return jnp.concatenate([ref[0, i] for i in range(4)], axis=1)


def local_kernel(fields_ref, dx_ref, dzt_ref, out_ref):
    nz = fields_ref.shape[3]
    nx = fields_ref.shape[2]
    dx = split_parts(dx_ref[...])
    dzt = split_parts(dzt_ref[...])
    fields = wide(fields_ref)
    sx = dot_parts(dx, split_parts(fields))
    sz = dot_parts(split_parts(jnp.concatenate([fields_ref[0, 0], fields_ref[0, 3]], axis=0)), dzt)
    sp, su, sv, sw = (sx[:, i * nz:(i + 1) * nz] for i in range(4))
    out_ref[0, 0] = fields_ref[0, 0] - time_step * (mach_number * sp + su + sz[nx:])
    out_ref[0, 1] = fields_ref[0, 1] - time_step * (mach_number * su + sp)
    out_ref[0, 2] = fields_ref[0, 2] - (time_step * mach_number) * sv
    out_ref[0, 3] = fields_ref[0, 3] - time_step * (mach_number * sw + sz[:nx])


def filter_kernel(fields_ref, fx_ref, fzt_ref, out_ref):
    nz = fields_ref.shape[3]
    nx = fields_ref.shape[2]
    fx = split_parts(fx_ref[...])
    fzt = split_parts(fzt_ref[...])
    sx = dot_parts(fx, split_parts(wide(fields_ref)))
    sz = dot_parts(split_parts(jnp.concatenate([fields_ref[0, i] for i in range(4)], axis=0)), fzt)
    for i in range(4):
        out_ref[0, i] = fields_ref[0, i] + filter_weight * (sx[:, i * nz:(i + 1) * nz] + sz[i * nx:(i + 1) * nx])


def row_call(kernel, fields, mat_x, mat_zt):
    rows, count, nx, nz = fields.shape
    block = pl.BlockSpec((1, count, nx, nz), lambda i: (i, 0, 0, 0))
    return pl.pallas_call(
        kernel,
        grid=(rows,),
        in_specs=[block, pl.BlockSpec((nx, nx), lambda i: (0, 0)), pl.BlockSpec((nz, nz), lambda i: (0, 0))],
        out_specs=block,
        out_shape=jax.ShapeDtypeStruct(fields.shape, jnp.float32),
        cost_estimate=pl.CostEstimate(
            flops=6 * rows * count * nx * nz * (nx + nz), bytes_accessed=8 * fields.size, transcendentals=0
        ),
    )(fields, mat_x, mat_zt)


def chain(streams, slabs):
    side = math.isqrt(streams)
    path = list(range(streams))
    if side * side == streams:
        path = [r * side + (c if r % 2 == 0 else side - 1 - c) for r in range(side) for c in range(side)]
    place = [path.index(s) for s in range(streams)]
    order = []
    for k in range(slabs):
        order += [s * slabs + k for s in (path if k % 2 == 0 else path[::-1])]
    return place, order


def neighbour_rows(values, width, order, sections):
    rows = values.shape[0]
    total = len(order)
    axes = ("section", "stream", "slab")

    def shift(part, steps):
        pairs = []
        for section in range(sections):
            for g in range(total):
                if 0 <= g + steps < total:
                    pairs.append((section * total + order[g], section * total + order[g + steps]))
        return lax.ppermute(part, axes, pairs)

    if rows >= width:
        return shift(values[rows - width:], 1), shift(values[:width], -1)
    reach = -(-width // rows)
    before = jnp.concatenate([shift(values, d) for d in range(reach, 0, -1)], axis=0)
    after = jnp.concatenate([shift(values, -d) for d in range(1, reach + 1)], axis=0)
    return before[reach * rows - width:], after[:width]


def slope(values, dim):
    pads = [(0, 0)] * values.ndim
    pads[dim] = (1, 1)
    padded = jnp.pad(values, pads)
    length = values.shape[dim]
    return 0.5 * (
        lax.slice_in_dim(padded, 2, length + 2, axis=dim) - lax.slice_in_dim(padded, 0, length, axis=dim)
    )


def lamb(fields, before, after):
    u, v, w = fields[:, 1], fields[:, 2], fields[:, 3]
    rows = fields.shape[0]
    near = jnp.concatenate([before, jnp.stack([u, w], axis=1), after], axis=0)
    c2 = 0.5 * (near[2:] - near[:rows])
    ox = c2[:, 1] - slope(v, 2)
    oy = slope(u, 2) - slope(w, 1)
    oz = slope(v, 1) - c2[:, 0]
    return jnp.stack([oy * w - oz * v, oz * u - ox * w, ox * v - oy * u], axis=1)


def shift_masked(value, dim, step):
    size = value.shape[dim]
    moved = pltpu.roll(value, (-step) % size, dim)
    index = lax.broadcasted_iota(jnp.int32, value.shape, dim)
    return jnp.where(index == (size - 1 if step > 0 else 0), 0.0, moved)


def inner_slope(value, dim):
    return 0.5 * (shift_masked(value, dim, 1) - shift_masked(value, dim, -1))


def fold(index, side):
    row = index // side
    col = index % side
    return row * side + col + (row % 2) * (side - 1 - 2 * col)


def steps_kernel(streams, slabs, cells_ref, region_ref, dx_ref, dzt_ref, fx_ref, fzt_ref, out_ref,
                 pv, uw, edge, part, source, forcing, dxs, dzs, fxs, fzs, pv_send, pv_recv, uw_send, uw_recv, src_send, src_recv, row_send, row_recv, in_send, in_recv, credit):
    _, _, rows, _, width, nz = cells_ref.shape
    nx = width * streams
    total = streams * slabs
    side = math.isqrt(streams)
    side = side if side * side == streams else streams
    section, stream, slab = lax.axis_index("section"), lax.axis_index("stream"), lax.axis_index("slab")

    def turn(place, which):
        return place + (which % 2) * (streams - 1 - 2 * place)

    def device_at(spot):
        which = spot // streams
        return (section, fold(turn(spot % streams, which), side), which)

    spot = slab * streams + turn(fold(stream, side), slab)
    has_low, has_high = spot > 0, spot < total - 1
    low = device_at(jnp.maximum(spot - 1, 0))
    high = device_at(jnp.minimum(spot + 1, total - 1))
    partner = (1 - section, stream, slab)
    is_flow, is_sound = section == 0, section == 1
    pairs = SEGMENTS // 2

    def remote(src, dst, send, recv, device):
        return pltpu.make_async_remote_copy(
            src_ref=src, dst_ref=dst, send_sem=send, recv_sem=recv,
            device_id=device, device_id_type=pl.DeviceIdType.MESH,
        )

    def axial(which):
        return pl.ds(pl.multiple_of(which * width, width), width)

    def pv_up(slot, piece):
        cut = axial(piece)
        return remote(
            pv.at[slot, pl.ds(rows, 2), :, cut], pv.at[slot, pl.ds(0, 2), :, cut],
            pv_send.at[slot, 0, piece], pv_recv.at[slot, 0, piece], high,
        )

    def pv_down(slot, piece):
        cut = axial(piece)
        return remote(
            pv.at[slot, pl.ds(2, 2), :, cut], pv.at[slot, pl.ds(rows + 2, 2), :, cut],
            pv_send.at[slot, 1, piece], pv_recv.at[slot, 1, piece], low,
        )

    def uw_up():
        return remote(uw.at[rows], uw.at[0], uw_send.at[0], uw_recv.at[0], high)

    def uw_down():
        return remote(uw.at[1], uw.at[rows + 1], uw_send.at[1], uw_recv.at[1], low)

    def src_copy():
        return remote(source, forcing, src_send, src_recv, partner)

    def start_both(up, down):
        @pl.when(has_high)
        def _():
            up.start()

        @pl.when(has_low)
        def _():
            down.start()

    def wait_both(up, down):
        @pl.when(has_low)
        def _():
            up.wait_recv()
            down.wait_send()

        @pl.when(has_high)
        def _():
            down.wait_recv()
            up.wait_send()

    def repeat(count, body):
        def step(i, carry):
            body(i)
            return carry

        lax.fori_loop(0, count, step, 0)

    def each_row(body):
        repeat(rows, body)

    for slot in range(2):
        for line in range(2):
            pv[slot, line] = jnp.zeros((2, nx, nz), jnp.float32)
            pv[slot, rows + 2 + line] = jnp.zeros((2, nx, nz), jnp.float32)
    uw[0] = jnp.zeros((2, nx, nz), jnp.float32)
    uw[rows + 1] = jnp.zeros((2, nx, nz), jnp.float32)

    barrier = pltpu.get_barrier_semaphore()

    def greet(device):
        pl.semaphore_signal(barrier, inc=1, device_id=device, device_id_type=pl.DeviceIdType.MESH)

    greet(partner)
    for t in range(1, streams):
        greet((section, (stream + t) % streams, slab))
    low_apart = has_low & (spot % streams == 0)
    high_apart = has_high & (spot % streams == streams - 1)

    @pl.when(low_apart)
    def _():
        greet(low)

    @pl.when(high_apart)
    def _():
        greet(high)

    pl.semaphore_wait(barrier, streams + low_apart.astype(jnp.int32) + high_apart.astype(jnp.int32))

    def chunk_of(which):
        return turn(fold(which, side), slab)

    def held(kind, which):
        target = (pv.at[0, pl.ds(2, rows)], uw.at[pl.ds(1, rows)])[kind]
        return target.at[:, :, axial(which)]

    def in_copy(kind, t):
        peer = (stream + t) % streams
        return remote(
            cells_ref.at[chunk_of(peer), kind], held(kind, stream),
            in_send.at[kind, t - 1], in_recv.at[kind, t - 1], (section, peer, slab),
        )

    def in_wait(kind, t):
        sender = (stream + streams - t) % streams
        landed = held(kind, sender)
        in_copy(kind, t).wait_send()
        remote(landed, landed, in_send.at[kind, t - 1], in_recv.at[kind, t - 1], (section, sender, slab)).wait_recv()

    def start_piece(slot, piece):
        start_both(pv_up(slot, piece), pv_down(slot, piece))

    for kind in range(2):
        for t in range(1, streams):
            in_copy(kind, t).start()
    own = chunk_of(stream)
    pv[0, 2:rows + 2, :, axial(stream)] = cells_ref[own, 0]
    uw[1:rows + 1, :, axial(stream)] = cells_ref[own, 1]
    start_piece(0, stream)
    dxs[0], dxs[1] = split_parts(dx_ref[...])
    dzs[0], dzs[1] = split_parts(dzt_ref[...])
    fxs[0], fxs[1] = split_parts(fx_ref[...])
    fzs[0], fzs[1] = split_parts(fzt_ref[...])
    for t in range(1, streams):
        in_wait(0, t)
        start_piece(0, (stream + streams - t) % streams)
    for t in range(1, streams):
        in_wait(1, t)

    @pl.when(is_flow)
    def _():
        start_both(uw_up(), uw_down())

    def operators(slot):
        def body(row):
            p, v, u, w = pv[slot, row + 2, 0], pv[slot, row + 2, 1], uw[row + 1, 0], uw[row + 1, 1]
            sx = dot_parts((dxs[0], dxs[1]), split_parts(jnp.concatenate([p, u, v, w], axis=1)))
            sz = dot_parts(split_parts(jnp.concatenate([p, w], axis=0)), (dzs[0], dzs[1]))
            sp, su, sv, sw = (sx[:, i * nz:(i + 1) * nz] for i in range(4))
            pv[1 - slot, row + 2, 0] = p - time_step * (mach_number * sp + su + sz[nx:])
            pv[1 - slot, row + 2, 1] = v - (time_step * mach_number) * sv
            uw[row + 1, 0] = u - time_step * (mach_number * su + sp)
            uw[row + 1, 1] = w - time_step * (mach_number * sw + sz[:nx])

        each_row(body)

    def add_forcing(slot):
        def body(row):
            uw[row + 1, 0] = uw[row + 1, 0] + time_step * forcing[row, 0]
            pv[1 - slot, row + 2, 1] = pv[1 - slot, row + 2, 1] + time_step * forcing[row, 1]
            uw[row + 1, 1] = uw[row + 1, 1] + time_step * forcing[row, 2]

        each_row(body)

    def update_pv(slot, send):
        def one(piece):
            cut = axial(piece)
            wait_both(pv_up(slot, piece), pv_down(slot, piece))

            def body(row):
                def dy(field):
                    ahead = pv[slot, row + 3, field, cut] - pv[slot, row + 1, field, cut]
                    return (8.0 * ahead - (pv[slot, row + 4, field, cut] - pv[slot, row, field, cut])) / 12.0

                pv[1 - slot, row + 2, 0, cut] = pv[1 - slot, row + 2, 0, cut] - time_step * dy(1)
                pv[1 - slot, row + 2, 1, cut] = pv[1 - slot, row + 2, 1, cut] - time_step * dy(0)

            each_row(body)

            def onward():
                edge[0, cut] = pv[slot, 1, 0, cut]
                edge[1, cut] = pv[slot, rows + 2, 0, cut]
                start_piece(1 - slot, piece)

            if send is None:
                onward()
            else:
                pl.when(send)(onward)

        repeat(streams, one)

    def lamb_rows():
        def body(row):
            u, v, w = uw[row + 1, 0], pv[0, row + 2, 1], uw[row + 1, 1]
            ox = 0.5 * (uw[row + 2, 1] - uw[row, 1]) - inner_slope(v, 1)
            oy = inner_slope(u, 1) - inner_slope(w, 0)
            oz = inner_slope(v, 0) - 0.5 * (uw[row + 2, 0] - uw[row, 0])
            mask = -region_ref[row]
            source[row, 0] = mask * (oy * w - oz * v)
            source[row, 1] = mask * (oz * u - ox * w)
            source[row, 2] = mask * (ox * v - oy * u)

        each_row(body)

    def advance_edges():
        def body(which):
            row = which * (rows + 1)
            p, u, w = edge[which], uw[row, 0], uw[row, 1]
            sx = dot_parts((dxs[0], dxs[1]), split_parts(jnp.concatenate([p, u, w], axis=1)))
            sz = dot_parts(split_parts(p), (dzs[0], dzs[1]))
            sp, su, sw = (sx[:, i * nz:(i + 1) * nz] for i in range(3))
            uw[row, 0] = u - time_step * (mach_number * su + sp)
            uw[row, 1] = w - time_step * (mach_number * sw + sz)

        @pl.when(is_flow)
        def _():
            repeat(2, body)

    def smooth(kind):
        def body(row):
            group = ((pv[0, row + 2, 0], pv[0, row + 2, 1]), (uw[row + 1, 0], uw[row + 1, 1]))[kind]
            sx = dot_parts((fxs[0], fxs[1]), split_parts(jnp.concatenate(group, axis=1)))
            sz = dot_parts(split_parts(jnp.concatenate(group, axis=0)), (fzs[0], fzs[1]))
            for i in range(2):
                part[kind, row, i] = group[i] + filter_weight * (sx[:, i * nz:(i + 1) * nz] + sz[i * nx:(i + 1) * nx])
            for t in range(1, streams):
                row_copy(kind, t, row).start()
            out_ref[own, kind, row] = part[kind, row, :, axial(stream)]

        each_row(body)

    def row_copy(kind, t, row):
        peer = (stream + t) % streams
        return remote(
            part.at[kind, row, :, axial(peer)], out_ref.at[own, kind, row],
            row_send.at[kind, t - 1, row], row_recv.at[kind, t - 1, row], (section, peer, slab),
        )

    def pair(m):
        last = m == pairs - 1

        @pl.when(is_flow)
        def _():
            @pl.when(m == 0)
            def _():
                wait_both(uw_up(), uw_down())

            @pl.when(m > 0)
            def _():
                src_copy().wait_send()

            lamb_rows()

            @pl.when(m > 0)
            def _():
                pl.semaphore_wait(credit, 1)

            src_copy().start()

        operators(0)

        @pl.when(is_sound)
        def _():
            src_copy().wait_recv()
            add_forcing(0)

        update_pv(0, None)
        operators(1)

        @pl.when(is_sound)
        def _():
            add_forcing(1)

            @pl.when(m < pairs - 1)
            def _():
                pl.semaphore_signal(credit, inc=1, device_id=partner, device_id_type=pl.DeviceIdType.MESH)

        @pl.when(m < pairs - 1)
        def _():
            advance_edges()

        @pl.when(last)
        def _():
            smooth(1)

        update_pv(1, m < pairs - 1)

        @pl.when(m < pairs - 1)
        def _():
            advance_edges()

    repeat(pairs, pair)

    @pl.when(is_flow)
    def _():
        src_copy().wait_send()

    smooth(0)

    def finish(kind):
        def body(row):
            for t in range(1, streams):
                sender = (stream + streams - t) % streams
                landed = out_ref.at[chunk_of(sender), kind, row]
                row_copy(kind, t, row).wait_send()
                remote(
                    landed, landed, row_send.at[kind, t - 1, row], row_recv.at[kind, t - 1, row], (section, sender, slab)
                ).wait_recv()

        each_row(body)

    finish(1)
    finish(0)


def steps_call(streams, slabs, cells, region, deriv_x, deriv_zt, filter_x, filter_zt):
    _, _, rows, _, width, nz = cells.shape
    nx = width * streams
    f32 = jnp.float32
    dma = pltpu.SemaphoreType.DMA
    return pl.pallas_call(
        functools.partial(steps_kernel, streams, slabs),
        out_shape=jax.ShapeDtypeStruct(cells.shape, f32),
        in_specs=[pl.BlockSpec(memory_space=pltpu.VMEM)] * 6,
        out_specs=pl.BlockSpec(memory_space=pltpu.VMEM),
        scratch_shapes=[
            pltpu.VMEM((2, rows + 4, 2, nx, nz), f32),
            pltpu.VMEM((rows + 2, 2, nx, nz), f32),
            pltpu.VMEM((2, nx, nz), f32),
            pltpu.VMEM((2, rows, 2, nx, nz), f32),
            pltpu.VMEM((rows, 3, nx, nz), f32),
            pltpu.VMEM((rows, 3, nx, nz), f32),
            pltpu.VMEM((2, nx, nx), jnp.bfloat16),
            pltpu.VMEM((2, nz, nz), jnp.bfloat16),
            pltpu.VMEM((2, nx, nx), jnp.bfloat16),
            pltpu.VMEM((2, nz, nz), jnp.bfloat16),
            dma((2, 2, streams)), dma((2, 2, streams)), dma((2,)), dma((2,)), dma, dma,
            dma((2, streams - 1, rows)), dma((2, streams - 1, rows)), dma((2, streams - 1)), dma((2, streams - 1)),
            pltpu.SemaphoreType.REGULAR,
        ],
        compiler_params=pltpu.CompilerParams(
            collective_id=0, has_side_effects=True, vmem_limit_bytes=48 * 1024 * 1024
        ),
    )(cells, jnp.broadcast_to(region, (rows, nx, nz)), deriv_x, deriv_zt, filter_x, filter_zt)


def plain_steps(order, fields, region, deriv_x, deriv_zt, filter_x, filter_zt):
    rows = fields.shape[0]
    forcing = None
    for segment in range(SEGMENTS):
        pv = jnp.stack([fields[:, 0], fields[:, 2]], axis=1)
        before, after = neighbour_rows(pv, 2, order, 2)
        if segment % 2 == 0:
            uw = jnp.stack([fields[:, 1], fields[:, 3]], axis=1)
            low, high = neighbour_rows(uw, 1, order, 1)
            source = -region * lamb(fields, low, high)
            forcing = lax.ppermute(source, "section", [(0, 1)])
        part = row_call(local_kernel, fields, deriv_x, deriv_zt)
        near = jnp.concatenate([before, pv, after], axis=0)
        dy = (8.0 * (near[3:3 + rows] - near[1:1 + rows]) - (near[4:4 + rows] - near[:rows])) / 12.0
        fields = jnp.stack(
            [
                part[:, 0] - time_step * dy[:, 1],
                part[:, 1] + time_step * forcing[:, 0],
                part[:, 2] + time_step * (forcing[:, 1] - dy[:, 0]),
                part[:, 3] + time_step * forcing[:, 2],
            ],
            axis=1,
        )
    return row_call(filter_kernel, fields, filter_x, filter_zt)


def shards(state, source_mask, deriv_x, deriv_z, filter_x, filter_z):
    streams, slabs = lax.axis_size("stream"), lax.axis_size("slab")
    place, order = chain(streams, slabs)
    fields = state[0]
    count, width_x, width_y, nz = fields.shape
    nx = width_x * streams
    rows = width_y // streams
    even = lax.axis_index("slab") % 2 == 0
    back = [streams - 1 - p for p in place]

    blocks = source_mask.astype(jnp.float32)
    region = jnp.repeat(jnp.repeat(blocks, MBLK, axis=0), MBLK, axis=1).T
    mine = jnp.asarray(place)[lax.axis_index("stream")]
    mine = jnp.where(even, mine, streams - 1 - mine)
    region = lax.dynamic_slice_in_dim(region, mine * rows, rows, 0)[:, None, :, None]
    deriv_zt, filter_zt = deriv_z.T, filter_z.T

    mats = (deriv_x, deriv_zt, filter_x, filter_zt)
    if rows >= 2:
        cells = fields.reshape(count // 2, 2, width_x, streams, rows, nz).transpose(3, 1, 4, 0, 2, 5)
        cells = steps_call(streams, slabs, cells, region[:, 0], *mats)
        return cells.transpose(3, 1, 4, 0, 2, 5).reshape(1, count, width_x, width_y, nz)
    parts = fields.reshape(count, width_x, streams, rows, nz).transpose(2, 3, 0, 1, 4)
    parts = jnp.where(even, jnp.stack([parts[p] for p in place]), jnp.stack([parts[p] for p in back]))
    parts = lax.all_to_all(parts, "stream", split_axis=0, concat_axis=0, tiled=True)
    fields = parts.transpose(1, 2, 0, 3, 4).reshape(rows, count, nx, nz)
    fields = plain_steps(order, fields, region, *mats)

    parts = fields.reshape(rows, count, streams, width_x, nz).transpose(2, 0, 1, 3, 4)
    parts = lax.all_to_all(parts, "stream", split_axis=0, concat_axis=0, tiled=True)
    inv_place = [place.index(j) for j in range(streams)]
    inv_back = [back.index(j) for j in range(streams)]
    parts = jnp.where(even, jnp.stack([parts[p] for p in inv_place]), jnp.stack([parts[p] for p in inv_back]))
    return parts.transpose(2, 3, 0, 1, 4).reshape(1, count, width_x, width_y, nz)


def solution(mesh):
    placed = (P("section", None, "stream", "slab", None), P(None, "slab"), P(), P(), P(), P())
    return jax.shard_map(
        shards,
        mesh=mesh,
        in_specs=placed,
        out_specs=P("section", None, "stream", "slab", None),
        check_vma=False,
    )
```

```python
import functools
import math

import jax
import jax.numpy as jnp
from jax import lax
from jax.experimental import pallas as pl
from jax.experimental.pallas import tpu as pltpu
from jax.sharding import PartitionSpec as P

SEGMENTS = 8
MBLK = 16

mach_number = 0.5
time_step = 0.05
filter_weight = 0.25


def split_parts(value):
    high = value.astype(jnp.bfloat16)
    low = (value - high.astype(jnp.float32)).astype(jnp.bfloat16)
    return high, low


def dot_parts(left, right):
    dot = functools.partial(jnp.dot, preferred_element_type=jnp.float32)
    return dot(left[0], right[0]) + (dot(left[0], right[1]) + dot(left[1], right[0]))


def wide(ref):
    return jnp.concatenate([ref[0, i] for i in range(4)], axis=1)


def local_kernel(fields_ref, dx_ref, dzt_ref, out_ref):
    nz = fields_ref.shape[3]
    nx = fields_ref.shape[2]
    dx = split_parts(dx_ref[...])
    dzt = split_parts(dzt_ref[...])
    fields = wide(fields_ref)
    sx = dot_parts(dx, split_parts(fields))
    sz = dot_parts(split_parts(jnp.concatenate([fields_ref[0, 0], fields_ref[0, 3]], axis=0)), dzt)
    sp, su, sv, sw = (sx[:, i * nz:(i + 1) * nz] for i in range(4))
    out_ref[0, 0] = fields_ref[0, 0] - time_step * (mach_number * sp + su + sz[nx:])
    out_ref[0, 1] = fields_ref[0, 1] - time_step * (mach_number * su + sp)
    out_ref[0, 2] = fields_ref[0, 2] - (time_step * mach_number) * sv
    out_ref[0, 3] = fields_ref[0, 3] - time_step * (mach_number * sw + sz[:nx])


def filter_kernel(fields_ref, fx_ref, fzt_ref, out_ref):
    nz = fields_ref.shape[3]
    nx = fields_ref.shape[2]
    fx = split_parts(fx_ref[...])
    fzt = split_parts(fzt_ref[...])
    sx = dot_parts(fx, split_parts(wide(fields_ref)))
    sz = dot_parts(split_parts(jnp.concatenate([fields_ref[0, i] for i in range(4)], axis=0)), fzt)
    for i in range(4):
        out_ref[0, i] = fields_ref[0, i] + filter_weight * (sx[:, i * nz:(i + 1) * nz] + sz[i * nx:(i + 1) * nx])


def row_call(kernel, fields, mat_x, mat_zt):
    rows, count, nx, nz = fields.shape
    block = pl.BlockSpec((1, count, nx, nz), lambda i: (i, 0, 0, 0))
    return pl.pallas_call(
        kernel,
        grid=(rows,),
        in_specs=[block, pl.BlockSpec((nx, nx), lambda i: (0, 0)), pl.BlockSpec((nz, nz), lambda i: (0, 0))],
        out_specs=block,
        out_shape=jax.ShapeDtypeStruct(fields.shape, jnp.float32),
        cost_estimate=pl.CostEstimate(
            flops=6 * rows * count * nx * nz * (nx + nz), bytes_accessed=8 * fields.size, transcendentals=0
        ),
    )(fields, mat_x, mat_zt)


def chain(streams, slabs):
    side = math.isqrt(streams)
    path = list(range(streams))
    if side * side == streams:
        path = [r * side + (c if r % 2 == 0 else side - 1 - c) for r in range(side) for c in range(side)]
    place = [path.index(s) for s in range(streams)]
    order = []
    for k in range(slabs):
        order += [s * slabs + k for s in (path if k % 2 == 0 else path[::-1])]
    return place, order


def neighbour_rows(values, width, order, sections):
    rows = values.shape[0]
    total = len(order)
    axes = ("section", "stream", "slab")

    def shift(part, steps):
        pairs = []
        for section in range(sections):
            for g in range(total):
                if 0 <= g + steps < total:
                    pairs.append((section * total + order[g], section * total + order[g + steps]))
        return lax.ppermute(part, axes, pairs)

    if rows >= width:
        return shift(values[rows - width:], 1), shift(values[:width], -1)
    reach = -(-width // rows)
    before = jnp.concatenate([shift(values, d) for d in range(reach, 0, -1)], axis=0)
    after = jnp.concatenate([shift(values, -d) for d in range(1, reach + 1)], axis=0)
    return before[reach * rows - width:], after[:width]


def slope(values, dim):
    pads = [(0, 0)] * values.ndim
    pads[dim] = (1, 1)
    padded = jnp.pad(values, pads)
    length = values.shape[dim]
    return 0.5 * (
        lax.slice_in_dim(padded, 2, length + 2, axis=dim) - lax.slice_in_dim(padded, 0, length, axis=dim)
    )


def lamb(fields, before, after):
    u, v, w = fields[:, 1], fields[:, 2], fields[:, 3]
    rows = fields.shape[0]
    near = jnp.concatenate([before, jnp.stack([u, w], axis=1), after], axis=0)
    c2 = 0.5 * (near[2:] - near[:rows])
    ox = c2[:, 1] - slope(v, 2)
    oy = slope(u, 2) - slope(w, 1)
    oz = slope(v, 1) - c2[:, 0]
    return jnp.stack([oy * w - oz * v, oz * u - ox * w, ox * v - oy * u], axis=1)


def shift_masked(value, dim, step):
    size = value.shape[dim]
    moved = pltpu.roll(value, (-step) % size, dim)
    index = lax.broadcasted_iota(jnp.int32, value.shape, dim)
    return jnp.where(index == (size - 1 if step > 0 else 0), 0.0, moved)


def inner_slope(value, dim):
    return 0.5 * (shift_masked(value, dim, 1) - shift_masked(value, dim, -1))


def fold(index, side):
    row = index // side
    col = index % side
    return row * side + col + (row % 2) * (side - 1 - 2 * col)


def steps_kernel(streams, slabs, cells_ref, region_ref, dx_ref, dzt_ref, fx_ref, fzt_ref, out_ref,
                 pv, uw, edge, part, source, forcing, dxs, dzs, fxs, fzs, pv_send, pv_recv, uw_send, uw_recv, src_send, src_recv, row_send, row_recv,
                 in_send, in_recv, far_send, far_recv, credit, go):
    _, span, _, width, nz = cells_ref.shape
    nx = width * streams
    rows = span // streams
    half = span // 2
    side = math.isqrt(streams)
    section, stream, slab = lax.axis_index("section"), lax.axis_index("stream"), lax.axis_index("slab")
    is_flow, is_sound = section == 0, section == 1
    count = rows + (1 - section) * (span - rows)
    pairs = SEGMENTS // 2

    def turn(place, which):
        return place + (which % 2) * (streams - 1 - 2 * place)

    def chunk_of(which):
        return turn(fold(which, side), slab)

    own = chunk_of(stream)
    base = own * rows

    def chain_step(step):
        place = own + step
        inside = (place >= 0) & (place < streams)
        peer = fold(turn(jnp.clip(place, 0, streams - 1), slab), side)
        sound = jnp.where(inside, peer, stream)
        level = jnp.where(inside & is_sound, slab, slab + step)
        valid = (level >= 0) & (level < slabs)
        return (section, jnp.where(is_flow, stream, sound), jnp.clip(level, 0, slabs - 1)), valid

    low, has_low = chain_step(-1)
    high, has_high = chain_step(1)
    partner = (1 - section, stream, slab)

    def remote(src, dst, send, recv, device):
        return pltpu.make_async_remote_copy(
            src_ref=src, dst_ref=dst, send_sem=send, recv_sem=recv,
            device_id=device, device_id_type=pl.DeviceIdType.MESH,
        )

    def axial(which):
        return pl.ds(pl.multiple_of(which * width, width), width)

    def pv_up(slot, piece):
        cut = axial(piece)
        return remote(
            pv.at[slot, pl.ds(count, 2), :, cut], pv.at[slot, pl.ds(0, 2), :, cut],
            pv_send.at[slot, 0, piece], pv_recv.at[slot, 0, piece], high,
        )

    def pv_down(slot, piece):
        cut = axial(piece)
        return remote(
            pv.at[slot, pl.ds(2, 2), :, cut], pv.at[slot, pl.ds(count + 2, 2), :, cut],
            pv_send.at[slot, 1, piece], pv_recv.at[slot, 1, piece], low,
        )

    def uw_up():
        return remote(uw.at[span], uw.at[0], uw_send.at[0], uw_recv.at[0], high)

    def uw_down():
        return remote(uw.at[1], uw.at[span + 1], uw_send.at[1], uw_recv.at[1], low)

    def src_copy(slot):
        return remote(source, forcing.at[slot], src_send.at[slot], src_recv.at[slot], partner)

    def start_both(up, down):
        @pl.when(has_high)
        def _():
            up.start()

        @pl.when(has_low)
        def _():
            down.start()

    def wait_both(up, down):
        @pl.when(has_low)
        def _():
            up.wait_recv()
            down.wait_send()

        @pl.when(has_high)
        def _():
            down.wait_recv()
            up.wait_send()

    def repeat(start, stop, body):
        def step(i, carry):
            body(i)
            return carry

        lax.fori_loop(start, stop, step, 0)

    zero = jnp.zeros((2, nx, nz), jnp.float32)

    @pl.when(jnp.logical_not(has_low))
    def _():
        for slot in range(2):
            for line in range(2):
                pv[slot, line] = zero
        uw[0] = zero

    @pl.when(jnp.logical_not(has_high))
    def _():
        for slot in range(2):
            for line in range(2):
                pv[slot, count + 2 + line] = zero
        uw[count + 1] = zero

    barrier = pltpu.get_barrier_semaphore()

    def greet(device):
        pl.semaphore_signal(barrier, inc=1, device_id=device, device_id_type=pl.DeviceIdType.MESH)

    greet(partner)
    for t in range(1, streams):
        greet((section, (stream + t) % streams, slab))

    @pl.when(slab > 0)
    def _():
        greet((section, stream, slab - 1))

    @pl.when(slab < slabs - 1)
    def _():
        greet((section, stream, slab + 1))

    pl.semaphore_wait(barrier, streams + (slab > 0).astype(jnp.int32) + (slab < slabs - 1).astype(jnp.int32))

    def held(kind, which, first, lines):
        target = (pv.at[0, pl.ds(2 + first, lines)], uw.at[pl.ds(1 + first, lines)])[kind]
        return target.at[:, :, axial(which)]

    def landing(kind, which, first, lines, recv, sender):
        landed = held(kind, which, first, lines)
        return remote(landed, landed, recv, recv, (section, sender, slab))

    def start_piece(slot, piece):
        start_both(pv_up(slot, piece), pv_down(slot, piece))

    beside = (stream + 1 - 2 * (stream % 2), stream + 2 - 4 * (stream // 2))
    across = streams - 1 - stream

    def near_copy(kind, j):
        return remote(
            cells_ref.at[kind], held(kind, stream, 0, span),
            in_send.at[kind, j], in_recv.at[kind, j], (section, beside[j], slab),
        )

    def far_copy(kind, j):
        passed = held(kind, beside[j], j * half, half)
        return remote(passed, passed, far_send.at[kind, j], far_recv.at[kind, j], (section, beside[1 - j], slab))

    def split_matrices():
        dxs[0], dxs[1] = split_parts(dx_ref[...])
        dzs[0], dzs[1] = split_parts(dzt_ref[...])
        fxs[0], fxs[1] = split_parts(fx_ref[...])
        fzs[0], fzs[1] = split_parts(fzt_ref[...])

    @pl.when(is_flow)
    def _():
        for kind in range(2):
            for j in range(2):
                near_copy(kind, j).start()
        pv[0, 2:span + 2, :, axial(stream)] = cells_ref[0]
        uw[1:span + 1, :, axial(stream)] = cells_ref[1]
        start_piece(0, stream)
        split_matrices()
        for kind in range(2):
            for j in range(2):
                landing(kind, beside[j], 0, span, in_recv.at[kind, j], beside[j]).wait_recv()
                far_copy(kind, j).start()
                if kind == 0:
                    start_piece(0, beside[j])
        for kind in range(2):
            for j in range(2):
                landing(kind, across, j * half, half, far_recv.at[kind, j], beside[1 - j]).wait_recv()
            if kind == 0:
                start_piece(0, across)
        start_both(uw_up(), uw_down())
        pl.semaphore_signal(go, inc=1, device_id=partner, device_id_type=pl.DeviceIdType.MESH)
        for kind in range(2):
            for j in range(2):
                near_copy(kind, j).wait_send()
                far_copy(kind, j).wait_send()
        wait_both(uw_up(), uw_down())

    def in_copy(kind, t):
        peer = (stream + t) % streams
        return remote(
            cells_ref.at[kind, pl.ds(chunk_of(peer) * rows, rows)], held(kind, stream, 0, rows),
            in_send.at[kind, t - 1], in_recv.at[kind, t - 1], (section, peer, slab),
        )

    @pl.when(is_sound)
    def _():
        split_matrices()
        pv[0, 2:rows + 2, :, axial(stream)] = cells_ref[0, pl.ds(base, rows)]
        uw[1:rows + 1, :, axial(stream)] = cells_ref[1, pl.ds(base, rows)]
        pl.semaphore_wait(go, 1)
        for kind in range(2):
            for t in range(1, streams):
                in_copy(kind, t).start()
        start_piece(0, stream)
        for kind in range(2):
            for t in range(1, streams):
                sender = (stream + streams - t) % streams
                in_copy(kind, t).wait_send()
                landing(kind, sender, 0, rows, in_recv.at[kind, t - 1], sender).wait_recv()
                if kind == 0:
                    start_piece(0, sender)

    def slope_y(slot, row, field, cut):
        ahead = pv[slot, row + 3, field, cut] - pv[slot, row + 1, field, cut]
        return (8.0 * ahead - (pv[slot, row + 4, field, cut] - pv[slot, row, field, cut])) / 12.0

    def advance(slot, row, inner):
        p, v, u, w = pv[slot, row + 2, 0], pv[slot, row + 2, 1], uw[row + 1, 0], uw[row + 1, 1]
        sx = dot_parts((dxs[0], dxs[1]), split_parts(jnp.concatenate([p, u, v, w], axis=1)))
        sz = dot_parts(split_parts(jnp.concatenate([p, w], axis=0)), (dzs[0], dzs[1]))
        sp, su, sv, sw = (sx[:, i * nz:(i + 1) * nz] for i in range(4))
        rate_p = mach_number * sp + su + sz[nx:]
        rate_v = mach_number * sv
        if inner:
            everywhere = pl.ds(0, nx)
            rate_p = rate_p + slope_y(slot, row, 1, everywhere)
            rate_v = rate_v + slope_y(slot, row, 0, everywhere)
        pv[1 - slot, row + 2, 0] = p - time_step * rate_p
        pv[1 - slot, row + 2, 1] = v - time_step * rate_v
        uw[row + 1, 0] = u - time_step * (mach_number * su + sp)
        uw[row + 1, 1] = w - time_step * (mach_number * sw + sz[:nx])

    def rim(k):
        return k + (k // 2) * (count - 4)

    def rim_rows(slot):
        repeat(0, 4, lambda k: advance(slot, rim(k), False))

    def inner_rows(slot):
        repeat(2, count - 2, lambda row: advance(slot, row, True))

    def add_forcing(slot, held_in):
        def body(row):
            uw[row + 1, 0] = uw[row + 1, 0] + time_step * forcing[held_in, row, 0]
            pv[1 - slot, row + 2, 1] = pv[1 - slot, row + 2, 1] + time_step * forcing[held_in, row, 1]
            uw[row + 1, 1] = uw[row + 1, 1] + time_step * forcing[held_in, row, 2]

        repeat(0, rows, body)

    def finish_rim(slot, send):
        def one(piece):
            cut = axial(piece)
            wait_both(pv_up(slot, piece), pv_down(slot, piece))

            def body(k):
                row = rim(k)
                pv[1 - slot, row + 2, 0, cut] = pv[1 - slot, row + 2, 0, cut] - time_step * slope_y(slot, row, 1, cut)
                pv[1 - slot, row + 2, 1, cut] = pv[1 - slot, row + 2, 1, cut] - time_step * slope_y(slot, row, 0, cut)

            repeat(0, 4, body)

            @pl.when(send)
            def _():
                edge[0, cut] = pv[slot, 1, 0, cut]
                edge[1, cut] = pv[slot, count + 2, 0, cut]
                start_piece(1 - slot, piece)

        repeat(0, streams, one)

    def lamb_rows():
        def body(line):
            row = base + line
            u, v, w = uw[row + 1, 0], pv[0, row + 2, 1], uw[row + 1, 1]
            ox = 0.5 * (uw[row + 2, 1] - uw[row, 1]) - inner_slope(v, 1)
            oy = inner_slope(u, 1) - inner_slope(w, 0)
            oz = inner_slope(v, 0) - 0.5 * (uw[row + 2, 0] - uw[row, 0])
            mask = -region_ref[line]
            source[line, 0] = mask * (oy * w - oz * v)
            source[line, 1] = mask * (oz * u - ox * w)
            source[line, 2] = mask * (ox * v - oy * u)

        repeat(0, rows, body)

    def advance_edges():
        def body(which):
            row = which * (span + 1)
            p, u, w = edge[which], uw[row, 0], uw[row, 1]
            sx = dot_parts((dxs[0], dxs[1]), split_parts(jnp.concatenate([p, u, w], axis=1)))
            sz = dot_parts(split_parts(p), (dzs[0], dzs[1]))
            sp, su, sw = (sx[:, i * nz:(i + 1) * nz] for i in range(3))
            uw[row, 0] = u - time_step * (mach_number * su + sp)
            uw[row, 1] = w - time_step * (mach_number * sw + sz)

        @pl.when(is_flow)
        def _():
            repeat(0, 2, body)

    def smooth(kind):
        def body(row):
            group = ((pv[0, row + 2, 0], pv[0, row + 2, 1]), (uw[row + 1, 0], uw[row + 1, 1]))[kind]
            sx = dot_parts((fxs[0], fxs[1]), split_parts(jnp.concatenate(group, axis=1)))
            sz = dot_parts(split_parts(jnp.concatenate(group, axis=0)), (fzs[0], fzs[1]))
            for i in range(2):
                part[kind, row, i] = group[i] + filter_weight * (sx[:, i * nz:(i + 1) * nz] + sz[i * nx:(i + 1) * nx])
            for t in range(1, streams):
                row_copy(kind, t, row).start()
            out_ref[kind, base + row] = part[kind, row, :, axial(stream)]

        repeat(0, rows, body)

    def smooth_own():
        mine = axial(stream)

        def body(row):
            group = (pv[0, row + 2, 0], pv[0, row + 2, 1], uw[row + 1, 0], uw[row + 1, 1])
            here = [pv[0, row + 2, 0, mine], pv[0, row + 2, 1, mine], uw[row + 1, 0, mine], uw[row + 1, 1, mine]]
            sx = dot_parts((fxs[0, mine], fxs[1, mine]), split_parts(jnp.concatenate(group, axis=1)))
            sz = dot_parts(split_parts(jnp.concatenate(here, axis=0)), (fzs[0], fzs[1]))
            for i in range(4):
                out_ref[i // 2, row, i % 2] = here[i] + filter_weight * (
                    sx[:, i * nz:(i + 1) * nz] + sz[i * width:(i + 1) * width]
                )

        repeat(0, span, body)

    def row_copy(kind, t, row):
        peer = (stream + t) % streams
        return remote(
            part.at[kind, row, :, axial(peer)], out_ref.at[kind, base + row],
            row_send.at[kind, t - 1, row], row_recv.at[kind, t - 1, row], (section, peer, slab),
        )

    def pair(m):
        more = m < pairs - 1
        which = m % 2

        @pl.when(is_flow)
        def _():
            @pl.when(m > 0)
            def _():
                src_copy(1 - which).wait_send()

            lamb_rows()

            @pl.when(m > 1)
            def _():
                pl.semaphore_wait(credit, 1)

            src_copy(which).start()

        rim_rows(0)

        @pl.when(is_sound)
        def _():
            src_copy(which).wait_recv()
            add_forcing(0, which)

        finish_rim(0, True)
        inner_rows(0)
        rim_rows(1)

        @pl.when(is_sound)
        def _():
            add_forcing(1, which)

            @pl.when(m < pairs - 2)
            def _():
                pl.semaphore_signal(credit, inc=1, device_id=partner, device_id_type=pl.DeviceIdType.MESH)

            @pl.when(m == pairs - 1)
            def _():
                smooth(1)

        @pl.when(more)
        def _():
            advance_edges()

        finish_rim(1, more)
        inner_rows(1)

        @pl.when(more)
        def _():
            advance_edges()

    repeat(0, pairs, pair)

    @pl.when(is_flow)
    def _():
        src_copy((pairs - 1) % 2).wait_send()
        smooth_own()

    @pl.when(is_sound)
    def _():
        smooth(0)

        for kind in (1, 0):
            def body(row):
                for t in range(1, streams):
                    sender = (stream + streams - t) % streams
                    landed = out_ref.at[kind, chunk_of(sender) * rows + row]
                    row_copy(kind, t, row).wait_send()
                    remote(
                        landed, landed, row_send.at[kind, t - 1, row], row_recv.at[kind, t - 1, row], (section, sender, slab)
                    ).wait_recv()

            repeat(0, rows, body)


def steps_call(streams, slabs, cells, region, deriv_x, deriv_zt, filter_x, filter_zt):
    _, span, _, width, nz = cells.shape
    nx = width * streams
    rows = span // streams
    f32 = jnp.float32
    dma = pltpu.SemaphoreType.DMA
    return pl.pallas_call(
        functools.partial(steps_kernel, streams, slabs),
        out_shape=jax.ShapeDtypeStruct(cells.shape, f32),
        in_specs=[pl.BlockSpec(memory_space=pltpu.VMEM)] * 6,
        out_specs=pl.BlockSpec(memory_space=pltpu.VMEM),
        scratch_shapes=[
            pltpu.VMEM((2, span + 4, 2, nx, nz), f32),
            pltpu.VMEM((span + 2, 2, nx, nz), f32),
            pltpu.VMEM((2, nx, nz), f32),
            pltpu.VMEM((2, rows, 2, nx, nz), f32),
            pltpu.VMEM((rows, 3, nx, nz), f32),
            pltpu.VMEM((2, rows, 3, nx, nz), f32),
            pltpu.VMEM((2, nx, nx), jnp.bfloat16),
            pltpu.VMEM((2, nz, nz), jnp.bfloat16),
            pltpu.VMEM((2, nx, nx), jnp.bfloat16),
            pltpu.VMEM((2, nz, nz), jnp.bfloat16),
            dma((2, 2, streams)), dma((2, 2, streams)), dma((2,)), dma((2,)), dma((2,)), dma((2,)),
            dma((2, streams - 1, rows)), dma((2, streams - 1, rows)), dma((2, streams - 1)), dma((2, streams - 1)),
            dma((2, 2)), dma((2, 2)),
            pltpu.SemaphoreType.REGULAR, pltpu.SemaphoreType.REGULAR,
        ],
        compiler_params=pltpu.CompilerParams(
            collective_id=0, has_side_effects=True, vmem_limit_bytes=48 * 1024 * 1024
        ),
    )(cells, jnp.broadcast_to(region, (rows, nx, nz)), deriv_x, deriv_zt, filter_x, filter_zt)


def plain_steps(order, fields, region, deriv_x, deriv_zt, filter_x, filter_zt):
    rows = fields.shape[0]
    forcing = None
    for segment in range(SEGMENTS):
        pv = jnp.stack([fields[:, 0], fields[:, 2]], axis=1)
        before, after = neighbour_rows(pv, 2, order, 2)
        if segment % 2 == 0:
            uw = jnp.stack([fields[:, 1], fields[:, 3]], axis=1)
            low, high = neighbour_rows(uw, 1, order, 1)
            source = -region * lamb(fields, low, high)
            forcing = lax.ppermute(source, "section", [(0, 1)])
        part = row_call(local_kernel, fields, deriv_x, deriv_zt)
        near = jnp.concatenate([before, pv, after], axis=0)
        dy = (8.0 * (near[3:3 + rows] - near[1:1 + rows]) - (near[4:4 + rows] - near[:rows])) / 12.0
        fields = jnp.stack(
            [
                part[:, 0] - time_step * dy[:, 1],
                part[:, 1] + time_step * forcing[:, 0],
                part[:, 2] + time_step * (forcing[:, 1] - dy[:, 0]),
                part[:, 3] + time_step * forcing[:, 2],
            ],
            axis=1,
        )
    return row_call(filter_kernel, fields, filter_x, filter_zt)


def shards(state, source_mask, deriv_x, deriv_z, filter_x, filter_z):
    streams, slabs = lax.axis_size("stream"), lax.axis_size("slab")
    place, order = chain(streams, slabs)
    fields = state[0]
    count, width_x, width_y, nz = fields.shape
    nx = width_x * streams
    rows = width_y // streams
    even = lax.axis_index("slab") % 2 == 0
    back = [streams - 1 - p for p in place]

    blocks = source_mask.astype(jnp.float32)
    region = jnp.repeat(jnp.repeat(blocks, MBLK, axis=0), MBLK, axis=1).T
    mine = jnp.asarray(place)[lax.axis_index("stream")]
    mine = jnp.where(even, mine, streams - 1 - mine)
    region = lax.dynamic_slice_in_dim(region, mine * rows, rows, 0)[:, None, :, None]
    deriv_zt, filter_zt = deriv_z.T, filter_z.T

    mats = (deriv_x, deriv_zt, filter_x, filter_zt)
    if rows >= 4 and streams == 4:
        cells = fields.reshape(count // 2, 2, width_x, width_y, nz).transpose(1, 3, 0, 2, 4)
        cells = steps_call(streams, slabs, cells, region[:, 0], *mats)
        return cells.transpose(2, 0, 3, 1, 4).reshape(1, count, width_x, width_y, nz)
    parts = fields.reshape(count, width_x, streams, rows, nz).transpose(2, 3, 0, 1, 4)
    parts = jnp.where(even, jnp.stack([parts[p] for p in place]), jnp.stack([parts[p] for p in back]))
    parts = lax.all_to_all(parts, "stream", split_axis=0, concat_axis=0, tiled=True)
    fields = parts.transpose(1, 2, 0, 3, 4).reshape(rows, count, nx, nz)
    fields = plain_steps(order, fields, region, *mats)

    parts = fields.reshape(rows, count, streams, width_x, nz).transpose(2, 0, 1, 3, 4)
    parts = lax.all_to_all(parts, "stream", split_axis=0, concat_axis=0, tiled=True)
    inv_place = [place.index(j) for j in range(streams)]
    inv_back = [back.index(j) for j in range(streams)]
    parts = jnp.where(even, jnp.stack([parts[p] for p in inv_place]), jnp.stack([parts[p] for p in inv_back]))
    return parts.transpose(2, 3, 0, 1, 4).reshape(1, count, width_x, width_y, nz)


def solution(mesh):
    placed = (P("section", None, "stream", "slab", None), P(None, "slab"), P(), P(), P(), P())
    return jax.shard_map(
        shards,
        mesh=mesh,
        in_specs=placed,
        out_specs=P("section", None, "stream", "slab", None),
        check_vma=False,
    )
```

```python
import functools
import math

import jax
import jax.numpy as jnp
from jax import lax
from jax.experimental import pallas as pl
from jax.experimental.pallas import tpu as pltpu
from jax.sharding import PartitionSpec as P

SEGMENTS = 8
MBLK = 16

mach_number = 0.5
time_step = 0.05
near_weight = 8.0 * time_step / 12.0
far_weight = time_step / 12.0
filter_weight = 0.25


def split_parts(value):
    high = value.astype(jnp.bfloat16)
    low = (value - high.astype(jnp.float32)).astype(jnp.bfloat16)
    return high, low


def dot_parts(left, right):
    dot = functools.partial(jnp.dot, preferred_element_type=jnp.float32)
    return dot(left[0], right[0]) + (dot(left[0], right[1]) + dot(left[1], right[0]))


def wide(ref):
    return jnp.concatenate([ref[0, i] for i in range(4)], axis=1)


def local_kernel(fields_ref, dx_ref, dzt_ref, out_ref):
    nz = fields_ref.shape[3]
    nx = fields_ref.shape[2]
    dx = split_parts(dx_ref[...])
    dzt = split_parts(dzt_ref[...])
    fields = wide(fields_ref)
    sx = dot_parts(dx, split_parts(fields))
    sz = dot_parts(split_parts(jnp.concatenate([fields_ref[0, 0], fields_ref[0, 3]], axis=0)), dzt)
    sp, su, sv, sw = (sx[:, i * nz:(i + 1) * nz] for i in range(4))
    out_ref[0, 0] = fields_ref[0, 0] - time_step * (mach_number * sp + su + sz[nx:])
    out_ref[0, 1] = fields_ref[0, 1] - time_step * (mach_number * su + sp)
    out_ref[0, 2] = fields_ref[0, 2] - (time_step * mach_number) * sv
    out_ref[0, 3] = fields_ref[0, 3] - time_step * (mach_number * sw + sz[:nx])


def filter_kernel(fields_ref, fx_ref, fzt_ref, out_ref):
    nz = fields_ref.shape[3]
    nx = fields_ref.shape[2]
    fx = split_parts(fx_ref[...])
    fzt = split_parts(fzt_ref[...])
    sx = dot_parts(fx, split_parts(wide(fields_ref)))
    sz = dot_parts(split_parts(jnp.concatenate([fields_ref[0, i] for i in range(4)], axis=0)), fzt)
    for i in range(4):
        out_ref[0, i] = fields_ref[0, i] + filter_weight * (sx[:, i * nz:(i + 1) * nz] + sz[i * nx:(i + 1) * nx])


def row_call(kernel, fields, mat_x, mat_zt):
    rows, count, nx, nz = fields.shape
    block = pl.BlockSpec((1, count, nx, nz), lambda i: (i, 0, 0, 0))
    return pl.pallas_call(
        kernel,
        grid=(rows,),
        in_specs=[block, pl.BlockSpec((nx, nx), lambda i: (0, 0)), pl.BlockSpec((nz, nz), lambda i: (0, 0))],
        out_specs=block,
        out_shape=jax.ShapeDtypeStruct(fields.shape, jnp.float32),
        cost_estimate=pl.CostEstimate(
            flops=6 * rows * count * nx * nz * (nx + nz), bytes_accessed=8 * fields.size, transcendentals=0
        ),
    )(fields, mat_x, mat_zt)


def chain(streams, slabs):
    side = math.isqrt(streams)
    path = list(range(streams))
    if side * side == streams:
        path = [r * side + (c if r % 2 == 0 else side - 1 - c) for r in range(side) for c in range(side)]
    place = [path.index(s) for s in range(streams)]
    order = []
    for k in range(slabs):
        order += [s * slabs + k for s in (path if k % 2 == 0 else path[::-1])]
    return place, order


def neighbour_rows(values, width, order, sections):
    rows = values.shape[0]
    total = len(order)
    axes = ("section", "stream", "slab")

    def shift(part, steps):
        pairs = []
        for section in range(sections):
            for g in range(total):
                if 0 <= g + steps < total:
                    pairs.append((section * total + order[g], section * total + order[g + steps]))
        return lax.ppermute(part, axes, pairs)

    if rows >= width:
        return shift(values[rows - width:], 1), shift(values[:width], -1)
    reach = -(-width // rows)
    before = jnp.concatenate([shift(values, d) for d in range(reach, 0, -1)], axis=0)
    after = jnp.concatenate([shift(values, -d) for d in range(1, reach + 1)], axis=0)
    return before[reach * rows - width:], after[:width]


def slope(values, dim):
    pads = [(0, 0)] * values.ndim
    pads[dim] = (1, 1)
    padded = jnp.pad(values, pads)
    length = values.shape[dim]
    return 0.5 * (
        lax.slice_in_dim(padded, 2, length + 2, axis=dim) - lax.slice_in_dim(padded, 0, length, axis=dim)
    )


def lamb(fields, before, after):
    u, v, w = fields[:, 1], fields[:, 2], fields[:, 3]
    rows = fields.shape[0]
    near = jnp.concatenate([before, jnp.stack([u, w], axis=1), after], axis=0)
    c2 = 0.5 * (near[2:] - near[:rows])
    ox = c2[:, 1] - slope(v, 2)
    oy = slope(u, 2) - slope(w, 1)
    oz = slope(v, 1) - c2[:, 0]
    return jnp.stack([oy * w - oz * v, oz * u - ox * w, ox * v - oy * u], axis=1)


def shift_masked(value, dim, step):
    size = value.shape[dim]
    moved = pltpu.roll(value, (-step) % size, dim)
    index = lax.broadcasted_iota(jnp.int32, value.shape, dim)
    return jnp.where(index == (size - 1 if step > 0 else 0), 0.0, moved)


def inner_slope(value, dim):
    return 0.5 * (shift_masked(value, dim, 1) - shift_masked(value, dim, -1))


def fold(index, side):
    row = index // side
    col = index % side
    return row * side + col + (row % 2) * (side - 1 - 2 * col)


def steps_kernel(streams, slabs, cells_ref, region_ref, dx_ref, dzt_ref, fx_ref, fzt_ref, out_ref,
                 pv, uw, ghost, part, source, forcing, dxs, dzs, fxs, fzs, pv_send, pv_recv, pass_send, uw_send, uw_recv, src_send, src_recv, row_send, row_recv,
                 in_send, in_recv, far_send, far_recv, credit, go, pass_free):
    _, span, _, width, nz = cells_ref.shape
    nx = width * streams
    rows = span // streams
    half = span // 2
    side = math.isqrt(streams)
    section, stream, slab = lax.axis_index("section"), lax.axis_index("stream"), lax.axis_index("slab")
    is_flow, is_sound = section == 0, section == 1
    count = rows + (1 - section) * (span - rows)
    pairs = SEGMENTS // 2

    def turn(place, which):
        return place + (which % 2) * (streams - 1 - 2 * place)

    def chunk_of(which):
        return turn(fold(which, side), slab)

    own = chunk_of(stream)
    base = own * rows

    def chain_step(step):
        place = own + step
        inside = (place >= 0) & (place < streams)
        peer = fold(turn(jnp.clip(place, 0, streams - 1), slab), side)
        sound = jnp.where(inside, peer, stream)
        level = jnp.where(inside & is_sound, slab, slab + step)
        valid = (level >= 0) & (level < slabs)
        return (section, jnp.where(is_flow, stream, sound), jnp.clip(level, 0, slabs - 1)), valid

    low, has_low = chain_step(-1)
    high, has_high = chain_step(1)
    partner = (1 - section, stream, slab)

    def remote(src, dst, send, recv, device):
        return pltpu.make_async_remote_copy(
            src_ref=src, dst_ref=dst, send_sem=send, recv_sem=recv,
            device_id=device, device_id_type=pl.DeviceIdType.MESH,
        )

    def axial(which):
        return pl.ds(pl.multiple_of(which * width, width), width)

    last = streams - 1
    at_start, at_end = own == 0, own == last
    relayed = streams // 2
    passes = is_flow & ((at_start & has_high) | (at_end & has_low))
    takes = is_flow & ((at_end & has_high) | (at_start & has_low))
    pass_side = at_start.astype(jnp.int32)
    mate = (section, fold(turn(jnp.where(at_start, last, 0), slab), side), slab)
    cut_level = jnp.where(at_end, high[2], low[2])
    cut_peer = (section, stream, cut_level)

    def pv_up(slot, deep, piece):
        cut = axial(piece)
        return remote(
            pv.at[slot, pl.ds(count - 2, 2), :, cut], ghost.at[deep, 0, :, :, cut],
            pv_send.at[deep, 0, piece], pv_recv.at[deep, 0, piece], high,
        )

    def pv_down(slot, deep, piece):
        cut = axial(piece)
        return remote(
            pv.at[slot, pl.ds(0, 2), :, cut], ghost.at[deep, 1, :, :, cut],
            pv_send.at[deep, 1, piece], pv_recv.at[deep, 1, piece], low,
        )

    outward = 2 * pass_side - 1
    across_peer = (section, mate[1], jnp.clip(slab + outward, 0, slabs - 1))
    giver = (section, mate[1], jnp.clip(slab - outward, 0, slabs - 1))

    def pass_on(slot, deep, piece):
        cut = axial(piece)
        edge_side = 1 - pass_side
        return remote(
            pv.at[slot, pl.ds(pass_side * (count - 2), 2), :, cut], ghost.at[deep, edge_side, :, :, cut],
            pass_send.at[deep, piece], pv_recv.at[deep, edge_side, piece], across_peer,
        )

    def uw_copy():
        return remote(
            uw.at[jnp.where(at_start, 1, span)], uw.at[jnp.where(at_start, span + 1, 0)], uw_send, uw_recv, cut_peer
        )

    def uw_landing():
        landed = uw.at[jnp.where(at_start, 0, span + 1)]
        return remote(landed, landed, uw_send, uw_recv, cut_peer)

    def src_copy(slot):
        return remote(source, forcing.at[slot], src_send.at[slot], src_recv.at[slot], partner)

    def sends_high(piece):
        return has_high & (is_sound | jnp.logical_not(at_end) | (piece >= relayed))

    def sends_low(piece):
        return has_low & (is_sound | jnp.logical_not(at_start) | (piece >= relayed))

    def start_piece(slot, deep, piece):
        @pl.when(passes & (piece < relayed))
        def _():
            pass_on(slot, deep, piece).start()

        @pl.when(sends_high(piece))
        def _():
            pv_up(slot, deep, piece).start()

        @pl.when(sends_low(piece))
        def _():
            pv_down(slot, deep, piece).start()

    def wait_piece(slot, deep, piece):
        @pl.when(has_low)
        def _():
            pv_up(slot, deep, piece).wait_recv()

        @pl.when(has_high)
        def _():
            pv_down(slot, deep, piece).wait_recv()

        @pl.when(passes & (piece < relayed))
        def _():
            pass_on(slot, deep, piece).wait_send()

        @pl.when(sends_high(piece))
        def _():
            pv_up(slot, deep, piece).wait_send()

        @pl.when(sends_low(piece))
        def _():
            pv_down(slot, deep, piece).wait_send()

    def repeat(start, stop, body):
        def step(i, carry):
            body(i)
            return carry

        lax.fori_loop(start, stop, step, 0)

    zero = jnp.zeros((2, nx, nz), jnp.float32)

    @pl.when(jnp.logical_not(has_low))
    def _():
        for deep in range(4):
            for line in range(2):
                ghost[deep, 0, line] = zero
        uw[0] = zero

    @pl.when(jnp.logical_not(has_high))
    def _():
        for deep in range(4):
            for line in range(2):
                ghost[deep, 1, line] = zero
        uw[count + 1] = zero

    barrier = pltpu.get_barrier_semaphore()

    def greet(device):
        pl.semaphore_signal(barrier, inc=1, device_id=device, device_id_type=pl.DeviceIdType.MESH)

    greet(partner)
    for t in range(1, streams):
        greet((section, (stream + t) % streams, slab))

    @pl.when(slab > 0)
    def _():
        greet((section, stream, slab - 1))

    @pl.when(slab < slabs - 1)
    def _():
        greet((section, stream, slab + 1))

    @pl.when(passes)
    def _():
        greet(across_peer)

    @pl.when(takes)
    def _():
        greet(giver)

    around = [slab > 0, slab < slabs - 1, passes, takes]
    pl.semaphore_wait(barrier, streams + sum(flag.astype(jnp.int32) for flag in around))

    def held(kind, which, first, lines):
        target = (pv.at[0, pl.ds(first, lines)], uw.at[pl.ds(1 + first, lines)])[kind]
        return target.at[:, :, axial(which)]

    def landing(kind, which, first, lines, recv, sender):
        landed = held(kind, which, first, lines)
        return remote(landed, landed, recv, recv, (section, sender, slab))

    beside = (stream + 1 - 2 * (stream % 2), stream + 2 - 4 * (stream // 2))
    across = streams - 1 - stream

    def near_copy(kind, j):
        return remote(
            cells_ref.at[kind], held(kind, stream, 0, span),
            in_send.at[kind, j], in_recv.at[kind, j], (section, beside[j], slab),
        )

    def far_copy(kind, j):
        passed = held(kind, beside[j], j * half, half)
        return remote(passed, passed, far_send.at[kind, j], far_recv.at[kind, j], (section, beside[1 - j], slab))

    def split_matrices():
        dxs[0], dxs[1] = split_parts(time_step * mach_number * dx_ref[...])
        fxs[0], fxs[1] = split_parts(filter_weight * fx_ref[...])
        for target, matrix in ((dzs, time_step * dzt_ref[...]), (fzs, filter_weight * fzt_ref[...])):
            high_part, low_part = split_parts(matrix)
            target[...] = jnp.concatenate(
                [
                    jnp.concatenate([high_part, low_part], axis=1),
                    jnp.concatenate([high_part, jnp.zeros_like(low_part)], axis=1),
                ],
                axis=0,
            )

    @pl.when(is_flow)
    def _():
        for kind in range(2):
            for j in range(2):
                near_copy(kind, j).start()
        pv[0, 0:span, :, axial(stream)] = cells_ref[0]
        uw[1:span + 1, :, axial(stream)] = cells_ref[1]
        start_piece(0, 0, stream)
        split_matrices()
        for kind in range(2):
            for j in range(2):
                landing(kind, beside[j], 0, span, in_recv.at[kind, j], beside[j]).wait_recv()
                far_copy(kind, j).start()
                if kind == 0:
                    start_piece(0, 0, beside[j])
        for kind in range(2):
            for j in range(2):
                landing(kind, across, j * half, half, far_recv.at[kind, j], beside[1 - j]).wait_recv()
            if kind == 0:
                start_piece(0, 0, across)
        pl.when(takes)(lambda: uw_copy().start())
        pl.semaphore_signal(go, inc=1, device_id=partner, device_id_type=pl.DeviceIdType.MESH)
        for kind in range(2):
            for j in range(2):
                near_copy(kind, j).wait_send()
                far_copy(kind, j).wait_send()

    def in_copy(kind, t):
        peer = (stream + t) % streams
        return remote(
            cells_ref.at[kind, pl.ds(chunk_of(peer) * rows, rows)], held(kind, stream, 0, rows),
            in_send.at[kind, t - 1], in_recv.at[kind, t - 1], (section, peer, slab),
        )

    @pl.when(is_sound)
    def _():
        split_matrices()
        pv[0, 0:rows, :, axial(stream)] = cells_ref[0, pl.ds(base, rows)]
        uw[1:rows + 1, :, axial(stream)] = cells_ref[1, pl.ds(base, rows)]
        pl.semaphore_wait(go, 1)
        for kind in range(2):
            for t in range(1, streams):
                in_copy(kind, t).start()
        start_piece(0, 0, stream)
        for kind in range(2):
            for t in range(1, streams):
                sender = (stream + streams - t) % streams
                in_copy(kind, t).wait_send()
                landing(kind, sender, 0, rows, in_recv.at[kind, t - 1], sender).wait_recv()
                if kind == 0:
                    start_piece(0, 0, sender)

    def along_x(mats, fields):
        upper = jnp.concatenate([h for h, l in fields], axis=1)
        lower = jnp.concatenate([l for h, l in fields], axis=1)
        result = dot_parts(mats, (upper, lower))
        return [result[:, i * nz:(i + 1) * nz] for i in range(len(fields))]

    def along_z(mats, fields):
        stacked = jnp.concatenate([jnp.concatenate(field, axis=1) for field in fields], axis=0)
        result = jnp.dot(stacked, mats, preferred_element_type=jnp.float32)
        result = result[:, :nz] + result[:, nz:]
        size = result.shape[0] // len(fields)
        return [result[i * size:(i + 1) * size] for i in range(len(fields))]

    def advance(slot, row, inner):
        p, v, u, w = pv[slot, row, 0], pv[slot, row, 1], uw[row + 1, 0], uw[row + 1, 1]
        fields = [split_parts(field) for field in (p, u, v, w)]
        sp, su, sv, sw = along_x((dxs[0], dxs[1]), fields)
        zp, zw = along_z(dzs[...], (fields[0], fields[3]))
        new_p = p - sp - (su + su) - zw
        new_v = v - sv
        if inner:
            def slope_y(field):
                ahead = pv[slot, row + 1, field] - pv[slot, row - 1, field]
                return near_weight * ahead - far_weight * (pv[slot, row + 2, field] - pv[slot, row - 2, field])

            new_p = new_p - slope_y(1)
            new_v = new_v - slope_y(0)
        pv[1 - slot, row, 0] = new_p
        pv[1 - slot, row, 1] = new_v
        uw[row + 1, 0] = u - su - (sp + sp)
        uw[row + 1, 1] = w - sw - zp

    def advance_two(slot, row, inner):
        advance(slot, row, inner)
        advance(slot, row + 1, inner)

    def rim_rows(slot):
        repeat(0, 2, lambda k: advance_two(slot, k * (count - 2), False))

    def inner_rows(slot, start, stop):
        limit = count // 2 - 1
        repeat(jnp.minimum(1 + start, limit), jnp.minimum(1 + stop, limit), lambda k: advance_two(slot, 2 * k, True))

    def add_forcing(slot, held_in):
        def body(row):
            uw[row + 1, 0] = uw[row + 1, 0] + time_step * forcing[held_in, row, 0]
            pv[1 - slot, row, 1] = pv[1 - slot, row, 1] + time_step * forcing[held_in, row, 1]
            uw[row + 1, 1] = uw[row + 1, 1] + time_step * forcing[held_in, row, 2]

        repeat(0, rows, body)

    def finish_rim(slot, deep, early, send, late):
        @pl.when(passes & late & send)
        def _():
            pl.semaphore_wait(pass_free, 1)

        def one(piece):
            cut = axial(piece)
            wait_piece(slot, deep, piece)

            for field in range(2):
                def line(row):
                    return pv[slot, row, field, cut]

                def below(which):
                    return ghost[deep, 0, which, field, cut]

                def above(which):
                    return ghost[deep, 1, which, field, cut]

                def change(row, near, far):
                    spot = pv.at[1 - slot, row, 1 - field, cut]
                    spot[...] = spot[...] - (near_weight * near - far_weight * far)

                change(0, line(1) - below(1), line(2) - below(0))
                change(1, line(2) - line(0), line(3) - below(1))
                change(count - 2, line(count - 1) - line(count - 3), above(0) - line(count - 4))
                change(count - 1, above(0) - line(count - 2), above(1) - line(count - 3))

            @pl.when(send)
            def _():
                start_piece(1 - slot, (deep + 1) % 4, piece)

        done = 0
        for piece in range(streams):
            goal = (span // 2 - 2) * (piece + 1) // streams
            inner_rows(slot, done, goal)
            done = goal
            one(piece)
        @pl.when(takes & send)
        def _():
            advance_edge(deep)

        @pl.when(takes & early)
        def _():
            pl.semaphore_signal(pass_free, inc=1, device_id=giver, device_id_type=pl.DeviceIdType.MESH)

    def advance_edge(deep):
        row = jnp.where(at_start, 0, span + 1)
        p, u, w = ghost[deep, 1 - pass_side, pass_side, 0], uw[row, 0], uw[row, 1]
        fields = [split_parts(field) for field in (p, u, w)]
        sp, su, sw = along_x((dxs[0], dxs[1]), fields)
        uw[row, 0] = u - su - (sp + sp)
        uw[row, 1] = w - sw - along_z(dzs[...], (fields[0],))[0]

    def lamb_rows():
        def body(line):
            row = base + line
            u, v, w = uw[row + 1, 0], pv[0, row, 1], uw[row + 1, 1]
            ox = 0.5 * (uw[row + 2, 1] - uw[row, 1]) - inner_slope(v, 1)
            oy = inner_slope(u, 1) - inner_slope(w, 0)
            oz = inner_slope(v, 0) - 0.5 * (uw[row + 2, 0] - uw[row, 0])
            mask = -region_ref[line]
            source[line, 0] = mask * (oy * w - oz * v)
            source[line, 1] = mask * (oz * u - ox * w)
            source[line, 2] = mask * (ox * v - oy * u)

        repeat(0, rows, body)

    def smooth(kind):
        def body(row):
            group = ((pv[0, row, 0], pv[0, row, 1]), (uw[row + 1, 0], uw[row + 1, 1]))[kind]
            fields = [split_parts(field) for field in group]
            sx = along_x((fxs[0], fxs[1]), fields)
            sz = along_z(fzs[...], fields)
            for i in range(2):
                part[kind, row, i] = group[i] + (sx[i] + sz[i])
            for t in range(1, streams):
                row_copy(kind, t, row).start()
            out_ref[kind, base + row] = part[kind, row, :, axial(stream)]

        repeat(0, rows, body)

    def smooth_own():
        mine = axial(stream)

        def body(row):
            group = (pv[0, row, 0], pv[0, row, 1], uw[row + 1, 0], uw[row + 1, 1])
            here = [pv[0, row, 0, mine], pv[0, row, 1, mine], uw[row + 1, 0, mine], uw[row + 1, 1, mine]]
            sx = along_x((fxs[0, mine], fxs[1, mine]), [split_parts(field) for field in group])
            sz = along_z(fzs[...], [split_parts(field) for field in here])
            for i in range(4):
                out_ref[i // 2, row, i % 2] = here[i] + (sx[i] + sz[i])

        repeat(0, span, body)

    def row_copy(kind, t, row):
        peer = (stream + t) % streams
        return remote(
            part.at[kind, row, :, axial(peer)], out_ref.at[kind, base + row],
            row_send.at[kind, t - 1, row], row_recv.at[kind, t - 1, row], (section, peer, slab),
        )

    def pair(m):
        more = m < pairs - 1
        which = m % 2
        deep = 2 * which

        @pl.when(is_flow)
        def _():
            @pl.when(takes & (m == 0))
            def _():
                uw_copy().wait_send()
                uw_landing().wait_recv()

            @pl.when(m > 0)
            def _():
                src_copy(1 - which).wait_send()

            lamb_rows()

            @pl.when(m > 1)
            def _():
                pl.semaphore_wait(credit, 1)

            src_copy(which).start()

        rim_rows(0)

        @pl.when(is_sound)
        def _():
            src_copy(which).wait_recv()
            add_forcing(0, which)

        finish_rim(0, deep, m < pairs - 2, True, m > 1)
        rim_rows(1)


        @pl.when(is_sound)
        def _():
            add_forcing(1, which)

            @pl.when(m < pairs - 2)
            def _():
                pl.semaphore_signal(credit, inc=1, device_id=partner, device_id_type=pl.DeviceIdType.MESH)

            @pl.when(m == pairs - 1)
            def _():
                smooth(1)

        finish_rim(1, deep + 1, m < pairs - 2, more, m > 0)
    repeat(0, pairs, pair)

    @pl.when(is_flow)
    def _():
        src_copy((pairs - 1) % 2).wait_send()
        smooth_own()

    @pl.when(is_sound)
    def _():
        smooth(0)

        for kind in (1, 0):
            def body(row):
                for t in range(1, streams):
                    sender = (stream + streams - t) % streams
                    landed = out_ref.at[kind, chunk_of(sender) * rows + row]
                    row_copy(kind, t, row).wait_send()
                    remote(
                        landed, landed, row_send.at[kind, t - 1, row], row_recv.at[kind, t - 1, row], (section, sender, slab)
                    ).wait_recv()

            repeat(0, rows, body)


def steps_call(streams, slabs, cells, region, deriv_x, deriv_zt, filter_x, filter_zt):
    _, span, _, width, nz = cells.shape
    nx = width * streams
    rows = span // streams
    f32 = jnp.float32
    dma = pltpu.SemaphoreType.DMA
    return pl.pallas_call(
        functools.partial(steps_kernel, streams, slabs),
        out_shape=jax.ShapeDtypeStruct(cells.shape, f32),
        in_specs=[pl.BlockSpec(memory_space=pltpu.VMEM)] * 6,
        out_specs=pl.BlockSpec(memory_space=pltpu.VMEM),
        scratch_shapes=[
            pltpu.VMEM((2, span, 2, nx, nz), f32),
            pltpu.VMEM((span + 2, 2, nx, nz), f32),
            pltpu.VMEM((4, 2, 2, 2, nx, nz), f32),
            pltpu.VMEM((2, rows, 2, nx, nz), f32),
            pltpu.VMEM((rows, 3, nx, nz), f32),
            pltpu.VMEM((2, rows, 3, nx, nz), f32),
            pltpu.VMEM((2, nx, nx), jnp.bfloat16),
            pltpu.VMEM((2 * nz, 2 * nz), jnp.bfloat16),
            pltpu.VMEM((2, nx, nx), jnp.bfloat16),
            pltpu.VMEM((2 * nz, 2 * nz), jnp.bfloat16),
            dma((4, 2, streams)), dma((4, 2, streams)), dma((4, streams)), dma, dma, dma((2,)), dma((2,)),
            dma((2, streams - 1, rows)), dma((2, streams - 1, rows)), dma((2, streams - 1)), dma((2, streams - 1)),
            dma((2, 2)), dma((2, 2)),
            pltpu.SemaphoreType.REGULAR, pltpu.SemaphoreType.REGULAR, pltpu.SemaphoreType.REGULAR,
        ],
        compiler_params=pltpu.CompilerParams(
            collective_id=0, has_side_effects=True, vmem_limit_bytes=48 * 1024 * 1024
        ),
    )(cells, jnp.broadcast_to(region, (rows, nx, nz)), deriv_x, deriv_zt, filter_x, filter_zt)


def plain_steps(order, fields, region, deriv_x, deriv_zt, filter_x, filter_zt):
    rows = fields.shape[0]
    forcing = None
    for segment in range(SEGMENTS):
        pv = jnp.stack([fields[:, 0], fields[:, 2]], axis=1)
        before, after = neighbour_rows(pv, 2, order, 2)
        if segment % 2 == 0:
            uw = jnp.stack([fields[:, 1], fields[:, 3]], axis=1)
            low, high = neighbour_rows(uw, 1, order, 1)
            source = -region * lamb(fields, low, high)
            forcing = lax.ppermute(source, "section", [(0, 1)])
        part = row_call(local_kernel, fields, deriv_x, deriv_zt)
        near = jnp.concatenate([before, pv, after], axis=0)
        dy = (8.0 * (near[3:3 + rows] - near[1:1 + rows]) - (near[4:4 + rows] - near[:rows])) / 12.0
        fields = jnp.stack(
            [
                part[:, 0] - time_step * dy[:, 1],
                part[:, 1] + time_step * forcing[:, 0],
                part[:, 2] + time_step * (forcing[:, 1] - dy[:, 0]),
                part[:, 3] + time_step * forcing[:, 2],
            ],
            axis=1,
        )
    return row_call(filter_kernel, fields, filter_x, filter_zt)


def shards(state, source_mask, deriv_x, deriv_z, filter_x, filter_z):
    streams, slabs = lax.axis_size("stream"), lax.axis_size("slab")
    place, order = chain(streams, slabs)
    fields = state[0]
    count, width_x, width_y, nz = fields.shape
    nx = width_x * streams
    rows = width_y // streams
    even = lax.axis_index("slab") % 2 == 0
    back = [streams - 1 - p for p in place]

    blocks = source_mask.astype(jnp.float32)
    region = jnp.repeat(jnp.repeat(blocks, MBLK, axis=0), MBLK, axis=1).T
    mine = jnp.asarray(place)[lax.axis_index("stream")]
    mine = jnp.where(even, mine, streams - 1 - mine)
    region = lax.dynamic_slice_in_dim(region, mine * rows, rows, 0)[:, None, :, None]
    deriv_zt, filter_zt = deriv_z.T, filter_z.T

    mats = (deriv_x, deriv_zt, filter_x, filter_zt)
    if rows >= 4 and streams == 4:
        cells = fields.reshape(count // 2, 2, width_x, width_y, nz).transpose(1, 3, 0, 2, 4)
        cells = steps_call(streams, slabs, cells, region[:, 0], *mats)
        return cells.transpose(2, 0, 3, 1, 4).reshape(1, count, width_x, width_y, nz)
    parts = fields.reshape(count, width_x, streams, rows, nz).transpose(2, 3, 0, 1, 4)
    parts = jnp.where(even, jnp.stack([parts[p] for p in place]), jnp.stack([parts[p] for p in back]))
    parts = lax.all_to_all(parts, "stream", split_axis=0, concat_axis=0, tiled=True)
    fields = parts.transpose(1, 2, 0, 3, 4).reshape(rows, count, nx, nz)
    fields = plain_steps(order, fields, region, *mats)

    parts = fields.reshape(rows, count, streams, width_x, nz).transpose(2, 0, 1, 3, 4)
    parts = lax.all_to_all(parts, "stream", split_axis=0, concat_axis=0, tiled=True)
    inv_place = [place.index(j) for j in range(streams)]
    inv_back = [back.index(j) for j in range(streams)]
    parts = jnp.where(even, jnp.stack([parts[p] for p in inv_place]), jnp.stack([parts[p] for p in inv_back]))
    return parts.transpose(2, 3, 0, 1, 4).reshape(1, count, width_x, width_y, nz)


def solution(mesh):
    placed = (P("section", None, "stream", "slab", None), P(None, "slab"), P(), P(), P(), P())
    return jax.shard_map(
        shards,
        mesh=mesh,
        in_specs=placed,
        out_specs=P("section", None, "stream", "slab", None),
        check_vma=False,
    )
```

```python
import functools
import math

import jax
import jax.numpy as jnp
from jax import lax
from jax.experimental import pallas as pl
from jax.experimental.pallas import tpu as pltpu
from jax.sharding import PartitionSpec as P

SEGMENTS = 8
MBLK = 16

mach_number = 0.5
time_step = 0.05
near_weight = 8.0 * time_step / 12.0
far_weight = time_step / 12.0
filter_weight = 0.25


def split_parts(value):
    high = value.astype(jnp.bfloat16)
    low = (value - high.astype(jnp.float32)).astype(jnp.bfloat16)
    return high, low


def dot_parts(left, right):
    dot = functools.partial(jnp.dot, preferred_element_type=jnp.float32)
    return dot(left[0], right[0]) + (dot(left[0], right[1]) + dot(left[1], right[0]))


def wide(ref):
    return jnp.concatenate([ref[0, i] for i in range(4)], axis=1)


def local_kernel(fields_ref, dx_ref, dz_ref, out_ref):
    nz = fields_ref.shape[3]
    nx = fields_ref.shape[2]
    dx = split_parts(dx_ref[...])
    dzt = split_parts(dz_ref[...])
    fields = wide(fields_ref)
    sx = dot_parts(dx, split_parts(fields))
    sz = dot_parts(split_parts(jnp.concatenate([fields_ref[0, 0], fields_ref[0, 3]], axis=0)), dzt)
    sp, su, sv, sw = (sx[:, i * nz:(i + 1) * nz] for i in range(4))
    out_ref[0, 0] = fields_ref[0, 0] - time_step * (mach_number * sp + su + sz[nx:])
    out_ref[0, 1] = fields_ref[0, 1] - time_step * (mach_number * su + sp)
    out_ref[0, 2] = fields_ref[0, 2] - (time_step * mach_number) * sv
    out_ref[0, 3] = fields_ref[0, 3] - time_step * (mach_number * sw + sz[:nx])


def filter_kernel(fields_ref, fx_ref, fz_ref, out_ref):
    nz = fields_ref.shape[3]
    nx = fields_ref.shape[2]
    fx = split_parts(fx_ref[...])
    fzt = split_parts(fz_ref[...])
    sx = dot_parts(fx, split_parts(wide(fields_ref)))
    sz = dot_parts(split_parts(jnp.concatenate([fields_ref[0, i] for i in range(4)], axis=0)), fzt)
    for i in range(4):
        out_ref[0, i] = fields_ref[0, i] + filter_weight * (sx[:, i * nz:(i + 1) * nz] + sz[i * nx:(i + 1) * nx])


def row_call(kernel, fields, mat_x, mat_zt):
    rows, count, nx, nz = fields.shape
    block = pl.BlockSpec((1, count, nx, nz), lambda i: (i, 0, 0, 0))
    return pl.pallas_call(
        kernel,
        grid=(rows,),
        in_specs=[block, pl.BlockSpec((nx, nx), lambda i: (0, 0)), pl.BlockSpec((nz, nz), lambda i: (0, 0))],
        out_specs=block,
        out_shape=jax.ShapeDtypeStruct(fields.shape, jnp.float32),
        cost_estimate=pl.CostEstimate(
            flops=6 * rows * count * nx * nz * (nx + nz), bytes_accessed=8 * fields.size, transcendentals=0
        ),
    )(fields, mat_x, mat_zt)


def chain(streams, slabs):
    side = math.isqrt(streams)
    path = list(range(streams))
    if side * side == streams:
        path = [r * side + (c if r % 2 == 0 else side - 1 - c) for r in range(side) for c in range(side)]
    place = [path.index(s) for s in range(streams)]
    order = []
    for k in range(slabs):
        order += [s * slabs + k for s in (path if k % 2 == 0 else path[::-1])]
    return place, order


def neighbour_rows(values, width, order, sections):
    rows = values.shape[0]
    total = len(order)
    axes = ("section", "stream", "slab")

    def shift(part, steps):
        pairs = []
        for section in range(sections):
            for g in range(total):
                if 0 <= g + steps < total:
                    pairs.append((section * total + order[g], section * total + order[g + steps]))
        return lax.ppermute(part, axes, pairs)

    if rows >= width:
        return shift(values[rows - width:], 1), shift(values[:width], -1)
    reach = -(-width // rows)
    before = jnp.concatenate([shift(values, d) for d in range(reach, 0, -1)], axis=0)
    after = jnp.concatenate([shift(values, -d) for d in range(1, reach + 1)], axis=0)
    return before[reach * rows - width:], after[:width]


def slope(values, dim):
    pads = [(0, 0)] * values.ndim
    pads[dim] = (1, 1)
    padded = jnp.pad(values, pads)
    length = values.shape[dim]
    return 0.5 * (
        lax.slice_in_dim(padded, 2, length + 2, axis=dim) - lax.slice_in_dim(padded, 0, length, axis=dim)
    )


def lamb(fields, before, after):
    u, v, w = fields[:, 1], fields[:, 2], fields[:, 3]
    rows = fields.shape[0]
    near = jnp.concatenate([before, jnp.stack([u, w], axis=1), after], axis=0)
    c2 = 0.5 * (near[2:] - near[:rows])
    ox = c2[:, 1] - slope(v, 2)
    oy = slope(u, 2) - slope(w, 1)
    oz = slope(v, 1) - c2[:, 0]
    return jnp.stack([oy * w - oz * v, oz * u - ox * w, ox * v - oy * u], axis=1)


def shift_masked(value, dim, step):
    size = value.shape[dim]
    moved = pltpu.roll(value, (-step) % size, dim)
    index = lax.broadcasted_iota(jnp.int32, value.shape, dim)
    return jnp.where(index == (size - 1 if step > 0 else 0), 0.0, moved)


def inner_slope(value, dim):
    return 0.5 * (shift_masked(value, dim, 1) - shift_masked(value, dim, -1))


def fold(index, side):
    row = index // side
    col = index % side
    return row * side + col + (row % 2) * (side - 1 - 2 * col)


def steps_kernel(streams, slabs, cells_ref, region_ref, dx_ref, dz_ref, fx_ref, fz_ref, out_ref,
                 pv, uw, ghost, part, source, forcing, dxs, dzs, fxs, fzs, pv_send, pv_recv, give_send, uw_send, uw_recv, src_send, src_recv, row_send, row_recv,
                 in_send, in_recv, far_send, far_recv, credit, go, give_free):
    _, span, _, width, nz = cells_ref.shape
    nx = width * streams
    rows = span // streams
    half = span // 2
    side = math.isqrt(streams)
    section, stream, slab = lax.axis_index("section"), lax.axis_index("stream"), lax.axis_index("slab")
    is_flow, is_sound = section == 0, section == 1
    count = rows + (1 - section) * (span - rows)
    pairs = SEGMENTS // 2

    def turn(place, which):
        return place + (which % 2) * (streams - 1 - 2 * place)

    def chunk_of(which):
        return turn(fold(which, side), slab)

    own = chunk_of(stream)
    base = own * rows

    def chain_step(step):
        place = own + step
        inside = (place >= 0) & (place < streams)
        peer = fold(turn(jnp.clip(place, 0, streams - 1), slab), side)
        sound = jnp.where(inside, peer, stream)
        level = jnp.where(inside & is_sound, slab, slab + step)
        valid = (level >= 0) & (level < slabs)
        return (section, jnp.where(is_flow, stream, sound), jnp.clip(level, 0, slabs - 1)), valid

    low, has_low = chain_step(-1)
    high, has_high = chain_step(1)
    partner = (1 - section, stream, slab)

    def remote(src, dst, send, recv, device):
        return pltpu.make_async_remote_copy(
            src_ref=src, dst_ref=dst, send_sem=send, recv_sem=recv,
            device_id=device, device_id_type=pl.DeviceIdType.MESH,
        )

    def axial(which):
        return pl.ds(pl.multiple_of(which * width, width), width)

    last = streams - 1
    at_start, at_end = own == 0, own == last
    takes = is_flow & ((at_end & has_high) | (at_start & has_low))
    edge_side = at_end.astype(jnp.int32)
    giving = (is_flow & has_high & jnp.logical_not(at_end), is_flow & has_low & jnp.logical_not(at_start))
    above_slab, below_slab = jnp.minimum(slab + 1, slabs - 1), jnp.maximum(slab - 1, 0)
    cut_chips = (
        (section, fold(turn(last, slab), side), above_slab),
        (section, fold(turn(0, slab), side), below_slab),
    )
    cut_level = jnp.where(at_end, high[2], low[2])
    cut_peer = (section, stream, cut_level)

    def pv_up(slot, deep, piece):
        cut = axial(piece)
        return remote(
            pv.at[slot, pl.ds(count - 2, 2), :, cut], ghost.at[deep, 0, :, :, cut],
            pv_send.at[deep, 0, piece], pv_recv.at[deep, 0, piece], high,
        )

    def pv_down(slot, deep, piece):
        cut = axial(piece)
        return remote(
            pv.at[slot, pl.ds(0, 2), :, cut], ghost.at[deep, 1, :, :, cut],
            pv_send.at[deep, 1, piece], pv_recv.at[deep, 1, piece], low,
        )

    def giver(t):
        return (section, (stream + t) % streams, jnp.where(at_end, above_slab, below_slab))

    def give(gap, slot, deep):
        cut = axial(stream)
        first = (count - 2, 0)[gap]
        return remote(
            pv.at[slot, pl.ds(first, 2), :, cut], ghost.at[deep, gap, :, :, cut],
            give_send.at[deep, gap], pv_recv.at[deep, gap, stream], cut_chips[gap],
        )

    def uw_copy():
        return remote(
            uw.at[jnp.where(at_start, 1, span)], uw.at[jnp.where(at_start, span + 1, 0)], uw_send, uw_recv, cut_peer
        )

    def uw_landing():
        landed = uw.at[jnp.where(at_start, 0, span + 1)]
        return remote(landed, landed, uw_send, uw_recv, cut_peer)

    def src_copy(slot):
        return remote(source, forcing.at[slot], src_send.at[slot], src_recv.at[slot], partner)

    def sends_high(piece):
        return has_high & (is_sound | jnp.logical_not(at_end) | (piece == stream))

    def sends_low(piece):
        return has_low & (is_sound | jnp.logical_not(at_start) | (piece == stream))

    def start_piece(slot, deep, piece):
        for gap in range(2):
            pl.when(giving[gap] & (piece == stream))(lambda: give(gap, slot, deep).start())

        @pl.when(sends_high(piece))
        def _():
            pv_up(slot, deep, piece).start()

        @pl.when(sends_low(piece))
        def _():
            pv_down(slot, deep, piece).start()

    def wait_piece(slot, deep, piece):
        @pl.when(has_low)
        def _():
            pv_up(slot, deep, piece).wait_recv()

        @pl.when(has_high)
        def _():
            pv_down(slot, deep, piece).wait_recv()

        for gap in range(2):
            pl.when(giving[gap] & (piece == stream))(lambda: give(gap, slot, deep).wait_send())

        @pl.when(sends_high(piece))
        def _():
            pv_up(slot, deep, piece).wait_send()

        @pl.when(sends_low(piece))
        def _():
            pv_down(slot, deep, piece).wait_send()

    def repeat(start, stop, body):
        def step(i, carry):
            body(i)
            return carry

        lax.fori_loop(start, stop, step, 0)

    zero = jnp.zeros((2, nx, nz), jnp.float32)

    @pl.when(jnp.logical_not(has_low))
    def _():
        for deep in range(4):
            for line in range(2):
                ghost[deep, 0, line] = zero
        uw[0] = zero

    @pl.when(jnp.logical_not(has_high))
    def _():
        for deep in range(4):
            for line in range(2):
                ghost[deep, 1, line] = zero
        uw[count + 1] = zero

    barrier = pltpu.get_barrier_semaphore()

    def greet(device):
        pl.semaphore_signal(barrier, inc=1, device_id=device, device_id_type=pl.DeviceIdType.MESH)

    greet(partner)
    for t in range(1, streams):
        greet((section, (stream + t) % streams, slab))

    @pl.when(slab > 0)
    def _():
        greet((section, stream, slab - 1))

    @pl.when(slab < slabs - 1)
    def _():
        greet((section, stream, slab + 1))

    for gap in range(2):
        pl.when(giving[gap])(lambda: greet(cut_chips[gap]))

    @pl.when(takes)
    def _():
        for t in range(1, streams):
            greet(giver(t))

    around = [slab > 0, slab < slabs - 1, giving[0], giving[1]] + [takes] * (streams - 1)
    pl.semaphore_wait(barrier, streams + sum(flag.astype(jnp.int32) for flag in around))

    def held(kind, which, first, lines):
        target = (pv.at[0, pl.ds(first, lines)], uw.at[pl.ds(1 + first, lines)])[kind]
        return target.at[:, :, axial(which)]

    def landing(kind, which, first, lines, recv, sender):
        landed = held(kind, which, first, lines)
        return remote(landed, landed, recv, recv, (section, sender, slab))

    beside = (stream + 1 - 2 * (stream % 2), stream + 2 - 4 * (stream // 2))
    across = streams - 1 - stream

    def near_copy(kind, j):
        return remote(
            cells_ref.at[kind], held(kind, stream, 0, span),
            in_send.at[kind, j], in_recv.at[kind, j], (section, beside[j], slab),
        )

    def far_copy(kind, j):
        passed = held(kind, beside[j], j * half, half)
        return remote(passed, passed, far_send.at[kind, j], far_recv.at[kind, j], (section, beside[1 - j], slab))

    def split_matrices():
        dxs[0], dxs[1] = split_parts(time_step * mach_number * dx_ref[...])
        fxs[0], fxs[1] = split_parts(filter_weight * fx_ref[...])
        for target, matrix in ((dzs, time_step * dz_ref[...].T), (fzs, filter_weight * fz_ref[...].T)):
            high_part, low_part = split_parts(matrix)
            target[...] = jnp.concatenate(
                [
                    jnp.concatenate([high_part, low_part], axis=1),
                    jnp.concatenate([high_part, jnp.zeros_like(low_part)], axis=1),
                ],
                axis=0,
            )

    @pl.when(is_flow)
    def _():
        for kind in range(2):
            for j in range(2):
                near_copy(kind, j).start()
        pv[0, 0:span, :, axial(stream)] = cells_ref[0]
        uw[1:span + 1, :, axial(stream)] = cells_ref[1]
        start_piece(0, 0, stream)
        split_matrices()
        for kind in range(2):
            for j in range(2):
                landing(kind, beside[j], 0, span, in_recv.at[kind, j], beside[j]).wait_recv()
                far_copy(kind, j).start()
                if kind == 0:
                    start_piece(0, 0, beside[j])
        for kind in range(2):
            for j in range(2):
                landing(kind, across, j * half, half, far_recv.at[kind, j], beside[1 - j]).wait_recv()
            if kind == 0:
                start_piece(0, 0, across)
        pl.when(takes)(lambda: uw_copy().start())
        pl.semaphore_signal(go, inc=1, device_id=partner, device_id_type=pl.DeviceIdType.MESH)
        for kind in range(2):
            for j in range(2):
                near_copy(kind, j).wait_send()
                far_copy(kind, j).wait_send()

    def in_copy(kind, t):
        peer = (stream + t) % streams
        return remote(
            cells_ref.at[kind, pl.ds(chunk_of(peer) * rows, rows)], held(kind, stream, 0, rows),
            in_send.at[kind, t - 1], in_recv.at[kind, t - 1], (section, peer, slab),
        )

    @pl.when(is_sound)
    def _():
        split_matrices()
        pv[0, 0:rows, :, axial(stream)] = cells_ref[0, pl.ds(base, rows)]
        uw[1:rows + 1, :, axial(stream)] = cells_ref[1, pl.ds(base, rows)]
        pl.semaphore_wait(go, 1)
        for kind in range(2):
            for t in range(1, streams):
                in_copy(kind, t).start()
        start_piece(0, 0, stream)
        for kind in range(2):
            for t in range(1, streams):
                sender = (stream + streams - t) % streams
                in_copy(kind, t).wait_send()
                landing(kind, sender, 0, rows, in_recv.at[kind, t - 1], sender).wait_recv()
                if kind == 0:
                    start_piece(0, 0, sender)

    def along_x(mats, fields):
        upper = jnp.concatenate([h for h, l in fields], axis=1)
        lower = jnp.concatenate([l for h, l in fields], axis=1)
        result = dot_parts(mats, (upper, lower))
        return [result[:, i * nz:(i + 1) * nz] for i in range(len(fields))]

    def along_z(mats, fields):
        stacked = jnp.concatenate([jnp.concatenate(field, axis=1) for field in fields], axis=0)
        result = jnp.dot(stacked, mats, preferred_element_type=jnp.float32)
        result = result[:, :nz] + result[:, nz:]
        size = result.shape[0] // len(fields)
        return [result[i * size:(i + 1) * size] for i in range(len(fields))]

    def advance(slot, row, inner):
        p, v, u, w = pv[slot, row, 0], pv[slot, row, 1], uw[row + 1, 0], uw[row + 1, 1]
        fields = [split_parts(field) for field in (p, u, v, w)]
        sp, su, sv, sw = along_x((dxs[0], dxs[1]), fields)
        zp, zw = along_z(dzs[...], (fields[0], fields[3]))
        new_p = p - sp - (su + su) - zw
        new_v = v - sv
        if inner:
            def slope_y(field):
                ahead = pv[slot, row + 1, field] - pv[slot, row - 1, field]
                return near_weight * ahead - far_weight * (pv[slot, row + 2, field] - pv[slot, row - 2, field])

            new_p = new_p - slope_y(1)
            new_v = new_v - slope_y(0)
        pv[1 - slot, row, 0] = new_p
        pv[1 - slot, row, 1] = new_v
        uw[row + 1, 0] = u - su - (sp + sp)
        uw[row + 1, 1] = w - sw - zp

    def advance_two(slot, row, inner):
        advance(slot, row, inner)
        advance(slot, row + 1, inner)

    def rim_rows(slot):
        repeat(0, 2, lambda k: advance_two(slot, k * (count - 2), False))

    def inner_rows(slot, start, stop):
        limit = count // 2 - 1
        repeat(jnp.minimum(1 + start, limit), jnp.minimum(1 + stop, limit), lambda k: advance_two(slot, 2 * k, True))

    def add_forcing(slot, held_in):
        def body(row):
            uw[row + 1, 0] = uw[row + 1, 0] + time_step * forcing[held_in, row, 0]
            pv[1 - slot, row, 1] = pv[1 - slot, row, 1] + time_step * forcing[held_in, row, 1]
            uw[row + 1, 1] = uw[row + 1, 1] + time_step * forcing[held_in, row, 2]

        repeat(0, rows, body)

    def finish_rim(slot, deep, early, send, late):
        for gap in range(2):
            pl.when(giving[gap] & late & send)(lambda: pl.semaphore_wait(give_free.at[gap], 1))

        def one(piece):
            cut = axial(piece)
            wait_piece(slot, deep, piece)

            for field in range(2):
                def line(row):
                    return pv[slot, row, field, cut]

                def below(which):
                    return ghost[deep, 0, which, field, cut]

                def above(which):
                    return ghost[deep, 1, which, field, cut]

                def change(row, near, far):
                    spot = pv.at[1 - slot, row, 1 - field, cut]
                    spot[...] = spot[...] - (near_weight * near - far_weight * far)

                change(0, line(1) - below(1), line(2) - below(0))
                change(1, line(2) - line(0), line(3) - below(1))
                change(count - 2, line(count - 1) - line(count - 3), above(0) - line(count - 4))
                change(count - 1, above(0) - line(count - 2), above(1) - line(count - 3))

            @pl.when(send)
            def _():
                start_piece(1 - slot, (deep + 1) % 4, piece)

        done = 0
        for piece in range(streams):
            goal = (span // 2 - 2) * (piece + 1) // streams
            inner_rows(slot, done, goal)
            done = goal
            one(piece)
        @pl.when(takes & send)
        def _():
            advance_edge(deep)

        @pl.when(takes & early)
        def _():
            for t in range(1, streams):
                pl.semaphore_signal(
                    give_free.at[edge_side], inc=1, device_id=giver(t), device_id_type=pl.DeviceIdType.MESH
                )

    def advance_edge(deep):
        row = jnp.where(at_start, 0, span + 1)
        p, u, w = ghost[deep, edge_side, 1 - edge_side, 0], uw[row, 0], uw[row, 1]
        fields = [split_parts(field) for field in (p, u, w)]
        sp, su, sw = along_x((dxs[0], dxs[1]), fields)
        uw[row, 0] = u - su - (sp + sp)
        uw[row, 1] = w - sw - along_z(dzs[...], (fields[0],))[0]

    def lamb_rows():
        def body(line):
            row = base + line
            u, v, w = uw[row + 1, 0], pv[0, row, 1], uw[row + 1, 1]
            ox = 0.5 * (uw[row + 2, 1] - uw[row, 1]) - inner_slope(v, 1)
            oy = inner_slope(u, 1) - inner_slope(w, 0)
            oz = inner_slope(v, 0) - 0.5 * (uw[row + 2, 0] - uw[row, 0])
            mask = -region_ref[line]
            source[line, 0] = mask * (oy * w - oz * v)
            source[line, 1] = mask * (oz * u - ox * w)
            source[line, 2] = mask * (ox * v - oy * u)

        repeat(0, rows, body)

    def smooth(kind):
        def body(row):
            group = ((pv[0, row, 0], pv[0, row, 1]), (uw[row + 1, 0], uw[row + 1, 1]))[kind]
            fields = [split_parts(field) for field in group]
            sx = along_x((fxs[0], fxs[1]), fields)
            sz = along_z(fzs[...], fields)
            for i in range(2):
                part[kind, row, i] = group[i] + (sx[i] + sz[i])
            for t in range(1, streams):
                row_copy(kind, t, row).start()
            out_ref[kind, base + row] = part[kind, row, :, axial(stream)]

        repeat(0, rows, body)

    def smooth_own():
        mine = axial(stream)

        def body(row):
            group = (pv[0, row, 0], pv[0, row, 1], uw[row + 1, 0], uw[row + 1, 1])
            here = [pv[0, row, 0, mine], pv[0, row, 1, mine], uw[row + 1, 0, mine], uw[row + 1, 1, mine]]
            sx = along_x((fxs[0, mine], fxs[1, mine]), [split_parts(field) for field in group])
            sz = along_z(fzs[...], [split_parts(field) for field in here])
            for i in range(4):
                out_ref[i // 2, row, i % 2] = here[i] + (sx[i] + sz[i])

        repeat(0, span, body)

    def row_copy(kind, t, row):
        peer = (stream + t) % streams
        return remote(
            part.at[kind, row, :, axial(peer)], out_ref.at[kind, base + row],
            row_send.at[kind, t - 1, row], row_recv.at[kind, t - 1, row], (section, peer, slab),
        )

    def pair(m):
        more = m < pairs - 1
        which = m % 2
        deep = 2 * which

        @pl.when(is_flow)
        def _():
            @pl.when(takes & (m == 0))
            def _():
                uw_copy().wait_send()
                uw_landing().wait_recv()

            @pl.when(m > 0)
            def _():
                src_copy(1 - which).wait_send()

            lamb_rows()

            @pl.when(m > 1)
            def _():
                pl.semaphore_wait(credit, 1)

            src_copy(which).start()

        rim_rows(0)

        @pl.when(is_sound)
        def _():
            src_copy(which).wait_recv()
            add_forcing(0, which)

        finish_rim(0, deep, m < pairs - 2, True, m > 1)
        rim_rows(1)


        @pl.when(is_sound)
        def _():
            add_forcing(1, which)

            @pl.when(m < pairs - 2)
            def _():
                pl.semaphore_signal(credit, inc=1, device_id=partner, device_id_type=pl.DeviceIdType.MESH)

            @pl.when(m == pairs - 1)
            def _():
                smooth(1)

        finish_rim(1, deep + 1, m < pairs - 2, more, m > 0)
    repeat(0, pairs, pair)

    @pl.when(is_flow)
    def _():
        src_copy((pairs - 1) % 2).wait_send()
        smooth_own()

    @pl.when(is_sound)
    def _():
        smooth(0)

        for kind in (1, 0):
            def body(row):
                for t in range(1, streams):
                    sender = (stream + streams - t) % streams
                    landed = out_ref.at[kind, chunk_of(sender) * rows + row]
                    row_copy(kind, t, row).wait_send()
                    remote(
                        landed, landed, row_send.at[kind, t - 1, row], row_recv.at[kind, t - 1, row], (section, sender, slab)
                    ).wait_recv()

            repeat(0, rows, body)


def steps_call(streams, slabs, cells, region, deriv_x, deriv_z, filter_x, filter_z):
    _, span, _, width, nz = cells.shape
    nx = width * streams
    rows = span // streams
    f32 = jnp.float32
    dma = pltpu.SemaphoreType.DMA
    return pl.pallas_call(
        functools.partial(steps_kernel, streams, slabs),
        out_shape=jax.ShapeDtypeStruct(cells.shape, f32),
        in_specs=[pl.BlockSpec(memory_space=pltpu.VMEM)] * 6,
        out_specs=pl.BlockSpec(memory_space=pltpu.VMEM),
        scratch_shapes=[
            pltpu.VMEM((2, span, 2, nx, nz), f32),
            pltpu.VMEM((span + 2, 2, nx, nz), f32),
            pltpu.VMEM((4, 2, 2, 2, nx, nz), f32),
            pltpu.VMEM((2, rows, 2, nx, nz), f32),
            pltpu.VMEM((rows, 3, nx, nz), f32),
            pltpu.VMEM((2, rows, 3, nx, nz), f32),
            pltpu.VMEM((2, nx, nx), jnp.bfloat16),
            pltpu.VMEM((2 * nz, 2 * nz), jnp.bfloat16),
            pltpu.VMEM((2, nx, nx), jnp.bfloat16),
            pltpu.VMEM((2 * nz, 2 * nz), jnp.bfloat16),
            dma((4, 2, streams)), dma((4, 2, streams)), dma((4, 2)), dma, dma, dma((2,)), dma((2,)),
            dma((2, streams - 1, rows)), dma((2, streams - 1, rows)), dma((2, streams - 1)), dma((2, streams - 1)),
            dma((2, 2)), dma((2, 2)),
            pltpu.SemaphoreType.REGULAR, pltpu.SemaphoreType.REGULAR, pltpu.SemaphoreType.REGULAR((2,)),
        ],
        compiler_params=pltpu.CompilerParams(
            collective_id=0, has_side_effects=True, vmem_limit_bytes=48 * 1024 * 1024
        ),
    )(cells, jnp.broadcast_to(region, (rows, nx, nz)), deriv_x, deriv_z, filter_x, filter_z)


def plain_steps(order, fields, region, deriv_x, deriv_zt, filter_x, filter_zt):
    rows = fields.shape[0]
    forcing = None
    for segment in range(SEGMENTS):
        pv = jnp.stack([fields[:, 0], fields[:, 2]], axis=1)
        before, after = neighbour_rows(pv, 2, order, 2)
        if segment % 2 == 0:
            uw = jnp.stack([fields[:, 1], fields[:, 3]], axis=1)
            low, high = neighbour_rows(uw, 1, order, 1)
            source = -region * lamb(fields, low, high)
            forcing = lax.ppermute(source, "section", [(0, 1)])
        part = row_call(local_kernel, fields, deriv_x, deriv_zt)
        near = jnp.concatenate([before, pv, after], axis=0)
        dy = (8.0 * (near[3:3 + rows] - near[1:1 + rows]) - (near[4:4 + rows] - near[:rows])) / 12.0
        fields = jnp.stack(
            [
                part[:, 0] - time_step * dy[:, 1],
                part[:, 1] + time_step * forcing[:, 0],
                part[:, 2] + time_step * (forcing[:, 1] - dy[:, 0]),
                part[:, 3] + time_step * forcing[:, 2],
            ],
            axis=1,
        )
    return row_call(filter_kernel, fields, filter_x, filter_zt)


def shards(state, source_mask, deriv_x, deriv_z, filter_x, filter_z):
    streams, slabs = lax.axis_size("stream"), lax.axis_size("slab")
    place, order = chain(streams, slabs)
    fields = state[0]
    count, width_x, width_y, nz = fields.shape
    nx = width_x * streams
    rows = width_y // streams
    even = lax.axis_index("slab") % 2 == 0
    back = [streams - 1 - p for p in place]

    blocks = source_mask.astype(jnp.float32)
    region = jnp.repeat(jnp.repeat(blocks, MBLK, axis=0), MBLK, axis=1).T
    mine = jnp.asarray(place)[lax.axis_index("stream")]
    mine = jnp.where(even, mine, streams - 1 - mine)
    region = lax.dynamic_slice_in_dim(region, mine * rows, rows, 0)[:, None, :, None]
    deriv_zt, filter_zt = deriv_z.T, filter_z.T

    mats = (deriv_x, deriv_zt, filter_x, filter_zt)
    if rows >= 4 and streams == 4:
        cells = fields.reshape(count // 2, 2, width_x, width_y, nz).transpose(1, 3, 0, 2, 4)
        cells = steps_call(streams, slabs, cells, region[:, 0], deriv_x, deriv_z, filter_x, filter_z)
        return cells.transpose(2, 0, 3, 1, 4).reshape(1, count, width_x, width_y, nz)
    parts = fields.reshape(count, width_x, streams, rows, nz).transpose(2, 3, 0, 1, 4)
    parts = jnp.where(even, jnp.stack([parts[p] for p in place]), jnp.stack([parts[p] for p in back]))
    parts = lax.all_to_all(parts, "stream", split_axis=0, concat_axis=0, tiled=True)
    fields = parts.transpose(1, 2, 0, 3, 4).reshape(rows, count, nx, nz)
    fields = plain_steps(order, fields, region, *mats)

    parts = fields.reshape(rows, count, streams, width_x, nz).transpose(2, 0, 1, 3, 4)
    parts = lax.all_to_all(parts, "stream", split_axis=0, concat_axis=0, tiled=True)
    inv_place = [place.index(j) for j in range(streams)]
    inv_back = [back.index(j) for j in range(streams)]
    parts = jnp.where(even, jnp.stack([parts[p] for p in inv_place]), jnp.stack([parts[p] for p in inv_back]))
    return parts.transpose(2, 3, 0, 1, 4).reshape(1, count, width_x, width_y, nz)


def solution(mesh):
    placed = (P("section", None, "stream", "slab", None), P(None, "slab"), P(), P(), P(), P())
    return jax.shard_map(
        shards,
        mesh=mesh,
        in_specs=placed,
        out_specs=P("section", None, "stream", "slab", None),
        check_vma=False,
    )
```

```python
import functools
import math

import jax
import jax.numpy as jnp
from jax import lax
from jax.experimental import pallas as pl
from jax.experimental.pallas import tpu as pltpu
from jax.sharding import PartitionSpec as P

SEGMENTS = 8
MBLK = 16

mach_number = 0.5
time_step = 0.05
near_weight = 8.0 * time_step / 12.0
far_weight = time_step / 12.0
filter_weight = 0.25


def split_parts(value):
    high = value.astype(jnp.bfloat16)
    low = (value - high.astype(jnp.float32)).astype(jnp.bfloat16)
    return high, low


def dot_parts(left, right):
    dot = functools.partial(jnp.dot, preferred_element_type=jnp.float32)
    return dot(left[0], right[0]) + (dot(left[0], right[1]) + dot(left[1], right[0]))


def wide(ref):
    return jnp.concatenate([ref[0, i] for i in range(4)], axis=1)


def local_kernel(fields_ref, dx_ref, dz_ref, out_ref):
    nz = fields_ref.shape[3]
    nx = fields_ref.shape[2]
    dx = split_parts(dx_ref[...])
    dzt = split_parts(dz_ref[...])
    fields = wide(fields_ref)
    sx = dot_parts(dx, split_parts(fields))
    sz = dot_parts(split_parts(jnp.concatenate([fields_ref[0, 0], fields_ref[0, 3]], axis=0)), dzt)
    sp, su, sv, sw = (sx[:, i * nz:(i + 1) * nz] for i in range(4))
    out_ref[0, 0] = fields_ref[0, 0] - time_step * (mach_number * sp + su + sz[nx:])
    out_ref[0, 1] = fields_ref[0, 1] - time_step * (mach_number * su + sp)
    out_ref[0, 2] = fields_ref[0, 2] - (time_step * mach_number) * sv
    out_ref[0, 3] = fields_ref[0, 3] - time_step * (mach_number * sw + sz[:nx])


def filter_kernel(fields_ref, fx_ref, fz_ref, out_ref):
    nz = fields_ref.shape[3]
    nx = fields_ref.shape[2]
    fx = split_parts(fx_ref[...])
    fzt = split_parts(fz_ref[...])
    sx = dot_parts(fx, split_parts(wide(fields_ref)))
    sz = dot_parts(split_parts(jnp.concatenate([fields_ref[0, i] for i in range(4)], axis=0)), fzt)
    for i in range(4):
        out_ref[0, i] = fields_ref[0, i] + filter_weight * (sx[:, i * nz:(i + 1) * nz] + sz[i * nx:(i + 1) * nx])


def row_call(kernel, fields, mat_x, mat_zt):
    rows, count, nx, nz = fields.shape
    block = pl.BlockSpec((1, count, nx, nz), lambda i: (i, 0, 0, 0))
    return pl.pallas_call(
        kernel,
        grid=(rows,),
        in_specs=[block, pl.BlockSpec((nx, nx), lambda i: (0, 0)), pl.BlockSpec((nz, nz), lambda i: (0, 0))],
        out_specs=block,
        out_shape=jax.ShapeDtypeStruct(fields.shape, jnp.float32),
        cost_estimate=pl.CostEstimate(
            flops=6 * rows * count * nx * nz * (nx + nz), bytes_accessed=8 * fields.size, transcendentals=0
        ),
    )(fields, mat_x, mat_zt)


def chain(streams, slabs):
    side = math.isqrt(streams)
    path = list(range(streams))
    if side * side == streams:
        path = [r * side + (c if r % 2 == 0 else side - 1 - c) for r in range(side) for c in range(side)]
    place = [path.index(s) for s in range(streams)]
    order = []
    for k in range(slabs):
        order += [s * slabs + k for s in (path if k % 2 == 0 else path[::-1])]
    return place, order


def neighbour_rows(values, width, order, sections):
    rows = values.shape[0]
    total = len(order)
    axes = ("section", "stream", "slab")

    def shift(part, steps):
        pairs = []
        for section in range(sections):
            for g in range(total):
                if 0 <= g + steps < total:
                    pairs.append((section * total + order[g], section * total + order[g + steps]))
        return lax.ppermute(part, axes, pairs)

    if rows >= width:
        return shift(values[rows - width:], 1), shift(values[:width], -1)
    reach = -(-width // rows)
    before = jnp.concatenate([shift(values, d) for d in range(reach, 0, -1)], axis=0)
    after = jnp.concatenate([shift(values, -d) for d in range(1, reach + 1)], axis=0)
    return before[reach * rows - width:], after[:width]


def slope(values, dim):
    pads = [(0, 0)] * values.ndim
    pads[dim] = (1, 1)
    padded = jnp.pad(values, pads)
    length = values.shape[dim]
    return 0.5 * (
        lax.slice_in_dim(padded, 2, length + 2, axis=dim) - lax.slice_in_dim(padded, 0, length, axis=dim)
    )


def lamb(fields, before, after):
    u, v, w = fields[:, 1], fields[:, 2], fields[:, 3]
    rows = fields.shape[0]
    near = jnp.concatenate([before, jnp.stack([u, w], axis=1), after], axis=0)
    c2 = 0.5 * (near[2:] - near[:rows])
    ox = c2[:, 1] - slope(v, 2)
    oy = slope(u, 2) - slope(w, 1)
    oz = slope(v, 1) - c2[:, 0]
    return jnp.stack([oy * w - oz * v, oz * u - ox * w, ox * v - oy * u], axis=1)


def shift_masked(value, dim, step):
    size = value.shape[dim]
    moved = pltpu.roll(value, (-step) % size, dim)
    index = lax.broadcasted_iota(jnp.int32, value.shape, dim)
    return jnp.where(index == (size - 1 if step > 0 else 0), 0.0, moved)


def inner_slope(value, dim):
    return 0.5 * (shift_masked(value, dim, 1) - shift_masked(value, dim, -1))


def fold(index, side):
    row = index // side
    col = index % side
    return row * side + col + (row % 2) * (side - 1 - 2 * col)


def steps_kernel(streams, slabs, cells_ref, region_ref, dx_ref, dz_ref, fx_ref, fz_ref, out_ref,
                 pv, uw, ghost, part, source, forcing, dxs, dzs, fxs, fzs, pv_send, pv_recv, give_send, uw_send, uw_recv, src_send, src_recv, row_send, row_recv,
                 in_send, in_recv, far_send, far_recv, credit, go, give_free, half_send, half_recv):
    _, span, _, width, nz = cells_ref.shape
    nx = width * streams
    rows = span // streams
    half = span // 2
    side = math.isqrt(streams)
    section, stream, slab = lax.axis_index("section"), lax.axis_index("stream"), lax.axis_index("slab")
    is_flow, is_sound = section == 0, section == 1
    count = rows + (1 - section) * (span - rows)
    pairs = SEGMENTS // 2

    def turn(place, which):
        return place + (which % 2) * (streams - 1 - 2 * place)

    def chunk_of(which):
        return turn(fold(which, side), slab)

    own = chunk_of(stream)
    base = own * rows

    def chain_step(step):
        place = own + step
        inside = (place >= 0) & (place < streams)
        peer = fold(turn(jnp.clip(place, 0, streams - 1), slab), side)
        sound = jnp.where(inside, peer, stream)
        level = jnp.where(inside & is_sound, slab, slab + step)
        valid = (level >= 0) & (level < slabs)
        return (section, jnp.where(is_flow, stream, sound), jnp.clip(level, 0, slabs - 1)), valid

    low, has_low = chain_step(-1)
    high, has_high = chain_step(1)
    partner = (1 - section, stream, slab)

    def remote(src, dst, send, recv, device):
        return pltpu.make_async_remote_copy(
            src_ref=src, dst_ref=dst, send_sem=send, recv_sem=recv,
            device_id=device, device_id_type=pl.DeviceIdType.MESH,
        )

    def axial(which):
        return pl.ds(pl.multiple_of(which * width, width), width)

    last = streams - 1
    at_start, at_end = own == 0, own == last
    takes = is_flow & ((at_end & has_high) | (at_start & has_low))
    edge_side = at_end.astype(jnp.int32)
    above_slab, below_slab = jnp.minimum(slab + 1, slabs - 1), jnp.maximum(slab - 1, 0)
    cut_chips = (
        (section, fold(turn(last, slab), side), above_slab),
        (section, fold(turn(0, slab), side), below_slab),
    )
    cut_level = jnp.where(at_end, high[2], low[2])
    cut_peer = (section, stream, cut_level)

    def pv_up(slot, deep, piece):
        cut = axial(piece)
        return remote(
            pv.at[slot, pl.ds(count - 2, 2), :, cut], ghost.at[deep, 0, :, :, cut],
            pv_send.at[deep, 0, piece], pv_recv.at[deep, 0, piece], high,
        )

    def pv_down(slot, deep, piece):
        cut = axial(piece)
        return remote(
            pv.at[slot, pl.ds(0, 2), :, cut], ghost.at[deep, 1, :, :, cut],
            pv_send.at[deep, 1, piece], pv_recv.at[deep, 1, piece], low,
        )

    has_side = (has_high, has_low)
    corner = streams - 1 - stream
    giving, helping = [], []
    for gap in range(2):
        target = cut_chips[gap][1]
        giving.append(is_flow & has_side[gap] & (stream != target) & (corner != target))
        helping.append(is_flow & has_side[gap] & (stream == target + 2 - 4 * (target // 2)))

    def giver(t):
        return (section, (stream + t) % streams, jnp.where(at_end, above_slab, below_slab))

    def half_of(piece, part):
        return pl.ds(pl.multiple_of(piece * width + part * (width // 2), width // 2), width // 2)

    def give(gap, slot, deep):
        cut = axial(stream)
        first = (count - 2, 0)[gap]
        return remote(
            pv.at[slot, pl.ds(first, 2), :, cut], ghost.at[deep, gap, :, :, cut],
            give_send.at[deep, gap, 0], pv_recv.at[deep, gap, stream], cut_chips[gap],
        )

    def give_half(gap, slot, deep, piece):
        cut = half_of(piece, 0)
        first = (count - 2, 0)[gap]
        return remote(
            pv.at[slot, pl.ds(first, 2), :, cut], ghost.at[deep, gap, :, :, cut],
            give_send.at[deep, gap, 1], pv_recv.at[deep, gap, piece], cut_chips[gap],
        )

    def cut_half(slot, deep):
        cut = half_of(corner, 1)
        return remote(
            pv.at[slot, pl.ds(edge_side * (count - 2), 2), :, cut], ghost.at[deep, 1 - edge_side, :, :, cut],
            half_send.at[deep], half_recv.at[deep], cut_peer,
        )

    def half_landing(deep, part):
        landed = ghost.at[deep, edge_side, :, :, half_of(corner, part)]
        semaphore = pv_recv.at[deep, edge_side, corner] if part == 0 else half_recv.at[deep]
        return remote(landed, landed, half_send.at[deep], semaphore, cut_peer)

    def uw_copy():
        return remote(
            uw.at[jnp.where(at_start, 1, span)], uw.at[jnp.where(at_start, span + 1, 0)], uw_send, uw_recv, cut_peer
        )

    def uw_landing():
        landed = uw.at[jnp.where(at_start, 0, span + 1)]
        return remote(landed, landed, uw_send, uw_recv, cut_peer)

    def src_copy(slot):
        return remote(source, forcing.at[slot], src_send.at[slot], src_recv.at[slot], partner)

    def sends_high(piece):
        return has_high & (is_sound | jnp.logical_not(at_end) | (piece == stream))

    def sends_low(piece):
        return has_low & (is_sound | jnp.logical_not(at_start) | (piece == stream))

    def start_piece(slot, deep, piece):
        for gap in range(2):
            pl.when(giving[gap] & (piece == stream))(lambda: give(gap, slot, deep).start())
            pl.when(helping[gap] & (piece == streams - 1 - cut_chips[gap][1]))(
                lambda: give_half(gap, slot, deep, piece).start()
            )
        pl.when(takes & (piece == corner))(lambda: cut_half(slot, deep).start())

        @pl.when(sends_high(piece))
        def _():
            pv_up(slot, deep, piece).start()

        @pl.when(sends_low(piece))
        def _():
            pv_down(slot, deep, piece).start()

    def wait_piece(slot, deep, piece):
        split = takes & (piece == corner)

        @pl.when(has_low & jnp.logical_not(split & at_start))
        def _():
            pv_up(slot, deep, piece).wait_recv()

        @pl.when(has_high & jnp.logical_not(split & at_end))
        def _():
            pv_down(slot, deep, piece).wait_recv()

        @pl.when(split)
        def _():
            half_landing(deep, 0).wait_recv()
            half_landing(deep, 1).wait_recv()

        for gap in range(2):
            pl.when(giving[gap] & (piece == stream))(lambda: give(gap, slot, deep).wait_send())
            pl.when(helping[gap] & (piece == streams - 1 - cut_chips[gap][1]))(
                lambda: give_half(gap, slot, deep, piece).wait_send()
            )
        pl.when(takes & (piece == corner))(lambda: cut_half(slot, deep).wait_send())

        @pl.when(sends_high(piece))
        def _():
            pv_up(slot, deep, piece).wait_send()

        @pl.when(sends_low(piece))
        def _():
            pv_down(slot, deep, piece).wait_send()

    def repeat(start, stop, body):
        def step(i, carry):
            body(i)
            return carry

        lax.fori_loop(start, stop, step, 0)

    barrier = pltpu.get_barrier_semaphore()

    def greet(device):
        pl.semaphore_signal(barrier, inc=1, device_id=device, device_id_type=pl.DeviceIdType.MESH)

    greet(partner)
    for t in range(1, streams):
        greet((section, (stream + t) % streams, slab))

    @pl.when(slab > 0)
    def _():
        greet((section, stream, slab - 1))

    @pl.when(slab < slabs - 1)
    def _():
        greet((section, stream, slab + 1))

    for gap in range(2):
        pl.when(giving[gap])(lambda: greet(cut_chips[gap]))

    @pl.when(takes)
    def _():
        for t in range(1, streams):
            pl.when((stream + t) % streams != corner)(lambda: greet(giver(t)))

    around = [slab > 0, slab < slabs - 1, giving[0], giving[1]] + [takes] * (streams - 2)
    pl.semaphore_wait(barrier, streams + sum(flag.astype(jnp.int32) for flag in around))

    def held(kind, which, first, lines):
        target = (pv.at[0, pl.ds(first, lines)], uw.at[pl.ds(1 + first, lines)])[kind]
        return target.at[:, :, axial(which)]

    def landing(kind, which, first, lines, recv, sender):
        landed = held(kind, which, first, lines)
        return remote(landed, landed, recv, recv, (section, sender, slab))

    beside = (stream + 1 - 2 * (stream % 2), stream + 2 - 4 * (stream // 2))
    across = streams - 1 - stream

    def near_copy(kind, j):
        return remote(
            cells_ref.at[kind], held(kind, stream, 0, span),
            in_send.at[kind, j], in_recv.at[kind, j], (section, beside[j], slab),
        )

    def far_copy(kind, j):
        passed = held(kind, beside[j], j * half, half)
        return remote(passed, passed, far_send.at[kind, j], far_recv.at[kind, j], (section, beside[1 - j], slab))

    def clear_ends():
        zero = jnp.zeros((2, nx, nz), jnp.float32)

        @pl.when(jnp.logical_not(has_low))
        def _():
            for deep in range(4):
                for line in range(2):
                    ghost[deep, 0, line] = zero
            uw[0] = zero

        @pl.when(jnp.logical_not(has_high))
        def _():
            for deep in range(4):
                for line in range(2):
                    ghost[deep, 1, line] = zero
            uw[count + 1] = zero

    def split_matrices():
        clear_ends()
        dxs[0], dxs[1] = split_parts(time_step * mach_number * dx_ref[...])
        fxs[0], fxs[1] = split_parts(filter_weight * fx_ref[...])
        for target, matrix in ((dzs, time_step * dz_ref[...].T), (fzs, filter_weight * fz_ref[...].T)):
            high_part, low_part = split_parts(matrix)
            target[...] = jnp.concatenate(
                [
                    jnp.concatenate([high_part, low_part], axis=1),
                    jnp.concatenate([high_part, jnp.zeros_like(low_part)], axis=1),
                ],
                axis=0,
            )

    @pl.when(is_flow)
    def _():
        for kind in range(2):
            for j in range(2):
                near_copy(kind, j).start()
        pv[0, 0:span, :, axial(stream)] = cells_ref[0]
        uw[1:span + 1, :, axial(stream)] = cells_ref[1]
        start_piece(0, 0, stream)
        split_matrices()
        for kind in range(2):
            for j in range(2):
                landing(kind, beside[j], 0, span, in_recv.at[kind, j], beside[j]).wait_recv()
                far_copy(kind, j).start()
                if kind == 0:
                    start_piece(0, 0, beside[j])
        for kind in range(2):
            for j in range(2):
                landing(kind, across, j * half, half, far_recv.at[kind, j], beside[1 - j]).wait_recv()
            if kind == 0:
                start_piece(0, 0, across)
        pl.when(takes)(lambda: uw_copy().start())
        pl.semaphore_signal(go, inc=1, device_id=partner, device_id_type=pl.DeviceIdType.MESH)
        for kind in range(2):
            for j in range(2):
                near_copy(kind, j).wait_send()
                far_copy(kind, j).wait_send()

    def in_copy(kind, t):
        peer = (stream + t) % streams
        return remote(
            cells_ref.at[kind, pl.ds(chunk_of(peer) * rows, rows)], held(kind, stream, 0, rows),
            in_send.at[kind, t - 1], in_recv.at[kind, t - 1], (section, peer, slab),
        )

    @pl.when(is_sound)
    def _():
        split_matrices()
        pv[0, 0:rows, :, axial(stream)] = cells_ref[0, pl.ds(base, rows)]
        uw[1:rows + 1, :, axial(stream)] = cells_ref[1, pl.ds(base, rows)]
        pl.semaphore_wait(go, 1)
        for kind in range(2):
            for t in range(1, streams):
                in_copy(kind, t).start()
        start_piece(0, 0, stream)
        for kind in range(2):
            for t in range(1, streams):
                sender = (stream + streams - t) % streams
                in_copy(kind, t).wait_send()
                landing(kind, sender, 0, rows, in_recv.at[kind, t - 1], sender).wait_recv()
                if kind == 0:
                    start_piece(0, 0, sender)

    def along_x(mats, fields):
        upper = jnp.concatenate([h for h, l in fields], axis=1)
        lower = jnp.concatenate([l for h, l in fields], axis=1)
        result = dot_parts(mats, (upper, lower))
        return [result[:, i * nz:(i + 1) * nz] for i in range(len(fields))]

    def along_z(mats, fields):
        stacked = jnp.concatenate([jnp.concatenate(field, axis=1) for field in fields], axis=0)
        result = jnp.dot(stacked, mats, preferred_element_type=jnp.float32)
        result = result[:, :nz] + result[:, nz:]
        size = result.shape[0] // len(fields)
        return [result[i * size:(i + 1) * size] for i in range(len(fields))]

    def advance(slot, row, inner):
        p, v, u, w = pv[slot, row, 0], pv[slot, row, 1], uw[row + 1, 0], uw[row + 1, 1]
        fields = [split_parts(field) for field in (p, u, v, w)]
        sp, su, sv, sw = along_x((dxs[0], dxs[1]), fields)
        zp, zw = along_z(dzs[...], (fields[0], fields[3]))
        new_p = p - sp - (su + su) - zw
        new_v = v - sv
        if inner:
            def slope_y(field):
                ahead = pv[slot, row + 1, field] - pv[slot, row - 1, field]
                return near_weight * ahead - far_weight * (pv[slot, row + 2, field] - pv[slot, row - 2, field])

            new_p = new_p - slope_y(1)
            new_v = new_v - slope_y(0)
        pv[1 - slot, row, 0] = new_p
        pv[1 - slot, row, 1] = new_v
        uw[row + 1, 0] = u - su - (sp + sp)
        uw[row + 1, 1] = w - sw - zp

    def advance_two(slot, row, inner):
        advance(slot, row, inner)
        advance(slot, row + 1, inner)

    def rim_rows(slot):
        repeat(0, 2, lambda k: advance_two(slot, k * (count - 2), False))

    def inner_rows(slot, start, stop):
        limit = count // 2 - 1
        repeat(jnp.minimum(1 + start, limit), jnp.minimum(1 + stop, limit), lambda k: advance_two(slot, 2 * k, True))

    def add_forcing(slot, held_in):
        def body(row):
            uw[row + 1, 0] = uw[row + 1, 0] + time_step * forcing[held_in, row, 0]
            pv[1 - slot, row, 1] = pv[1 - slot, row, 1] + time_step * forcing[held_in, row, 1]
            uw[row + 1, 1] = uw[row + 1, 1] + time_step * forcing[held_in, row, 2]

        repeat(0, rows, body)

    def finish_rim(slot, deep, early, send, late):
        for gap in range(2):
            pl.when(giving[gap] & late & send)(lambda: pl.semaphore_wait(give_free.at[gap], 1))

        def one(piece):
            cut = axial(piece)
            wait_piece(slot, deep, piece)

            for field in range(2):
                def line(row):
                    return pv[slot, row, field, cut]

                def below(which):
                    return ghost[deep, 0, which, field, cut]

                def above(which):
                    return ghost[deep, 1, which, field, cut]

                def change(row, near, far):
                    spot = pv.at[1 - slot, row, 1 - field, cut]
                    spot[...] = spot[...] - (near_weight * near - far_weight * far)

                change(0, line(1) - below(1), line(2) - below(0))
                change(1, line(2) - line(0), line(3) - below(1))
                change(count - 2, line(count - 1) - line(count - 3), above(0) - line(count - 4))
                change(count - 1, above(0) - line(count - 2), above(1) - line(count - 3))

            @pl.when(send)
            def _():
                start_piece(1 - slot, (deep + 1) % 4, piece)

        done = 0
        for piece in range(streams):
            goal = (span // 2 - 2) * (piece + 1) // streams
            inner_rows(slot, done, goal)
            done = goal
            one(piece)
        @pl.when(takes & send)
        def _():
            advance_edge(deep)

        @pl.when(takes & early)
        def _():
            for t in range(1, streams):
                @pl.when((stream + t) % streams != corner)
                def _():
                    pl.semaphore_signal(
                        give_free.at[edge_side], inc=1, device_id=giver(t), device_id_type=pl.DeviceIdType.MESH
                    )

    def advance_edge(deep):
        row = jnp.where(at_start, 0, span + 1)
        p, u, w = ghost[deep, edge_side, 1 - edge_side, 0], uw[row, 0], uw[row, 1]
        fields = [split_parts(field) for field in (p, u, w)]
        sp, su, sw = along_x((dxs[0], dxs[1]), fields)
        uw[row, 0] = u - su - (sp + sp)
        uw[row, 1] = w - sw - along_z(dzs[...], (fields[0],))[0]

    def lamb_rows():
        def body(line):
            row = base + line
            u, v, w = uw[row + 1, 0], pv[0, row, 1], uw[row + 1, 1]
            ox = 0.5 * (uw[row + 2, 1] - uw[row, 1]) - inner_slope(v, 1)
            oy = inner_slope(u, 1) - inner_slope(w, 0)
            oz = inner_slope(v, 0) - 0.5 * (uw[row + 2, 0] - uw[row, 0])
            mask = -region_ref[line]
            source[line, 0] = mask * (oy * w - oz * v)
            source[line, 1] = mask * (oz * u - ox * w)
            source[line, 2] = mask * (ox * v - oy * u)

        repeat(0, rows, body)

    def smooth(kind):
        def body(row):
            group = ((pv[0, row, 0], pv[0, row, 1]), (uw[row + 1, 0], uw[row + 1, 1]))[kind]
            fields = [split_parts(field) for field in group]
            sx = along_x((fxs[0], fxs[1]), fields)
            sz = along_z(fzs[...], fields)
            for i in range(2):
                part[kind, row, i] = group[i] + (sx[i] + sz[i])
            for t in range(1, streams):
                row_copy(kind, t, row).start()
            out_ref[kind, base + row] = part[kind, row, :, axial(stream)]

        repeat(0, rows, body)

    def smooth_own():
        mine = axial(stream)

        def body(row):
            group = (pv[0, row, 0], pv[0, row, 1], uw[row + 1, 0], uw[row + 1, 1])
            here = [pv[0, row, 0, mine], pv[0, row, 1, mine], uw[row + 1, 0, mine], uw[row + 1, 1, mine]]
            sx = along_x((fxs[0, mine], fxs[1, mine]), [split_parts(field) for field in group])
            sz = along_z(fzs[...], [split_parts(field) for field in here])
            for i in range(4):
                out_ref[i // 2, row, i % 2] = here[i] + (sx[i] + sz[i])

        repeat(0, span, body)

    def row_copy(kind, t, row):
        peer = (stream + t) % streams
        return remote(
            part.at[kind, row, :, axial(peer)], out_ref.at[kind, base + row],
            row_send.at[kind, t - 1, row], row_recv.at[kind, t - 1, row], (section, peer, slab),
        )

    def pair(m):
        more = m < pairs - 1
        which = m % 2
        deep = 2 * which

        @pl.when(is_flow)
        def _():
            @pl.when(takes & (m == 0))
            def _():
                uw_copy().wait_send()
                uw_landing().wait_recv()

            @pl.when(m > 0)
            def _():
                src_copy(1 - which).wait_send()

            lamb_rows()

            @pl.when(m > 1)
            def _():
                pl.semaphore_wait(credit, 1)

            src_copy(which).start()

        rim_rows(0)

        @pl.when(is_sound)
        def _():
            src_copy(which).wait_recv()
            add_forcing(0, which)

        finish_rim(0, deep, m < pairs - 2, True, m > 1)
        rim_rows(1)


        @pl.when(is_sound)
        def _():
            add_forcing(1, which)

            @pl.when(m < pairs - 2)
            def _():
                pl.semaphore_signal(credit, inc=1, device_id=partner, device_id_type=pl.DeviceIdType.MESH)

            @pl.when(m == pairs - 1)
            def _():
                smooth(1)

        finish_rim(1, deep + 1, m < pairs - 2, more, m > 0)
    repeat(0, pairs, pair)

    @pl.when(is_flow)
    def _():
        src_copy((pairs - 1) % 2).wait_send()
        smooth_own()

    @pl.when(is_sound)
    def _():
        smooth(0)

        for kind in (1, 0):
            def body(row):
                for t in range(1, streams):
                    sender = (stream + streams - t) % streams
                    landed = out_ref.at[kind, chunk_of(sender) * rows + row]
                    row_copy(kind, t, row).wait_send()
                    remote(
                        landed, landed, row_send.at[kind, t - 1, row], row_recv.at[kind, t - 1, row], (section, sender, slab)
                    ).wait_recv()

            repeat(0, rows, body)


def steps_call(streams, slabs, cells, region, deriv_x, deriv_z, filter_x, filter_z):
    _, span, _, width, nz = cells.shape
    nx = width * streams
    rows = span // streams
    f32 = jnp.float32
    dma = pltpu.SemaphoreType.DMA
    return pl.pallas_call(
        functools.partial(steps_kernel, streams, slabs),
        out_shape=jax.ShapeDtypeStruct(cells.shape, f32),
        in_specs=[pl.BlockSpec(memory_space=pltpu.VMEM)] * 6,
        out_specs=pl.BlockSpec(memory_space=pltpu.VMEM),
        scratch_shapes=[
            pltpu.VMEM((2, span, 2, nx, nz), f32),
            pltpu.VMEM((span + 2, 2, nx, nz), f32),
            pltpu.VMEM((4, 2, 2, 2, nx, nz), f32),
            pltpu.VMEM((2, rows, 2, nx, nz), f32),
            pltpu.VMEM((rows, 3, nx, nz), f32),
            pltpu.VMEM((2, rows, 3, nx, nz), f32),
            pltpu.VMEM((2, nx, nx), jnp.bfloat16),
            pltpu.VMEM((2 * nz, 2 * nz), jnp.bfloat16),
            pltpu.VMEM((2, nx, nx), jnp.bfloat16),
            pltpu.VMEM((2 * nz, 2 * nz), jnp.bfloat16),
            dma((4, 2, streams)), dma((4, 2, streams)), dma((4, 2, 2)), dma, dma, dma((2,)), dma((2,)),
            dma((2, streams - 1, rows)), dma((2, streams - 1, rows)), dma((2, streams - 1)), dma((2, streams - 1)),
            dma((2, 2)), dma((2, 2)),
            pltpu.SemaphoreType.REGULAR, pltpu.SemaphoreType.REGULAR, pltpu.SemaphoreType.REGULAR((2,)), dma((4,)), dma((4,)),
        ],
        compiler_params=pltpu.CompilerParams(
            collective_id=0, has_side_effects=True, vmem_limit_bytes=48 * 1024 * 1024
        ),
    )(cells, jnp.broadcast_to(region, (rows, nx, nz)), deriv_x, deriv_z, filter_x, filter_z)


def plain_steps(order, fields, region, deriv_x, deriv_zt, filter_x, filter_zt):
    rows = fields.shape[0]
    forcing = None
    for segment in range(SEGMENTS):
        pv = jnp.stack([fields[:, 0], fields[:, 2]], axis=1)
        before, after = neighbour_rows(pv, 2, order, 2)
        if segment % 2 == 0:
            uw = jnp.stack([fields[:, 1], fields[:, 3]], axis=1)
            low, high = neighbour_rows(uw, 1, order, 1)
            source = -region * lamb(fields, low, high)
            forcing = lax.ppermute(source, "section", [(0, 1)])
        part = row_call(local_kernel, fields, deriv_x, deriv_zt)
        near = jnp.concatenate([before, pv, after], axis=0)
        dy = (8.0 * (near[3:3 + rows] - near[1:1 + rows]) - (near[4:4 + rows] - near[:rows])) / 12.0
        fields = jnp.stack(
            [
                part[:, 0] - time_step * dy[:, 1],
                part[:, 1] + time_step * forcing[:, 0],
                part[:, 2] + time_step * (forcing[:, 1] - dy[:, 0]),
                part[:, 3] + time_step * forcing[:, 2],
            ],
            axis=1,
        )
    return row_call(filter_kernel, fields, filter_x, filter_zt)


def shards(state, source_mask, deriv_x, deriv_z, filter_x, filter_z):
    streams, slabs = lax.axis_size("stream"), lax.axis_size("slab")
    place, order = chain(streams, slabs)
    fields = state[0]
    count, width_x, width_y, nz = fields.shape
    nx = width_x * streams
    rows = width_y // streams
    even = lax.axis_index("slab") % 2 == 0
    back = [streams - 1 - p for p in place]

    blocks = source_mask.astype(jnp.float32)
    region = jnp.repeat(jnp.repeat(blocks, MBLK, axis=0), MBLK, axis=1).T
    mine = jnp.asarray(place)[lax.axis_index("stream")]
    mine = jnp.where(even, mine, streams - 1 - mine)
    region = lax.dynamic_slice_in_dim(region, mine * rows, rows, 0)[:, None, :, None]
    deriv_zt, filter_zt = deriv_z.T, filter_z.T

    mats = (deriv_x, deriv_zt, filter_x, filter_zt)
    if rows >= 4 and streams == 4:
        cells = fields.reshape(count // 2, 2, width_x, width_y, nz).transpose(1, 3, 0, 2, 4)
        cells = steps_call(streams, slabs, cells, region[:, 0], deriv_x, deriv_z, filter_x, filter_z)
        return cells.transpose(2, 0, 3, 1, 4).reshape(1, count, width_x, width_y, nz)
    parts = fields.reshape(count, width_x, streams, rows, nz).transpose(2, 3, 0, 1, 4)
    parts = jnp.where(even, jnp.stack([parts[p] for p in place]), jnp.stack([parts[p] for p in back]))
    parts = lax.all_to_all(parts, "stream", split_axis=0, concat_axis=0, tiled=True)
    fields = parts.transpose(1, 2, 0, 3, 4).reshape(rows, count, nx, nz)
    fields = plain_steps(order, fields, region, *mats)

    parts = fields.reshape(rows, count, streams, width_x, nz).transpose(2, 0, 1, 3, 4)
    parts = lax.all_to_all(parts, "stream", split_axis=0, concat_axis=0, tiled=True)
    inv_place = [place.index(j) for j in range(streams)]
    inv_back = [back.index(j) for j in range(streams)]
    parts = jnp.where(even, jnp.stack([parts[p] for p in inv_place]), jnp.stack([parts[p] for p in inv_back]))
    return parts.transpose(2, 3, 0, 1, 4).reshape(1, count, width_x, width_y, nz)


def solution(mesh):
    placed = (P("section", None, "stream", "slab", None), P(None, "slab"), P(), P(), P(), P())
    return jax.shard_map(
        shards,
        mesh=mesh,
        in_specs=placed,
        out_specs=P("section", None, "stream", "slab", None),
        check_vma=False,
    )
```

```python
import functools
import math

import jax
import jax.numpy as jnp
from jax import lax
from jax.experimental import pallas as pl
from jax.experimental.pallas import tpu as pltpu
from jax.sharding import PartitionSpec as P

SEGMENTS = 8
MBLK = 16

mach_number = 0.5
time_step = 0.05
near_weight = 8.0 * time_step / 12.0
far_weight = time_step / 12.0
filter_weight = 0.25


def split_parts(value):
    high = value.astype(jnp.bfloat16)
    low = (value - high.astype(jnp.float32)).astype(jnp.bfloat16)
    return high, low


def dot_parts(left, right):
    dot = functools.partial(jnp.dot, preferred_element_type=jnp.float32)
    return dot(left[0], right[0]) + (dot(left[0], right[1]) + dot(left[1], right[0]))


def wide(ref):
    return jnp.concatenate([ref[0, i] for i in range(4)], axis=1)


def local_kernel(fields_ref, dx_ref, dz_ref, out_ref):
    nz = fields_ref.shape[3]
    nx = fields_ref.shape[2]
    dx = split_parts(dx_ref[...])
    dzt = split_parts(dz_ref[...])
    fields = wide(fields_ref)
    sx = dot_parts(dx, split_parts(fields))
    sz = dot_parts(split_parts(jnp.concatenate([fields_ref[0, 0], fields_ref[0, 3]], axis=0)), dzt)
    sp, su, sv, sw = (sx[:, i * nz:(i + 1) * nz] for i in range(4))
    out_ref[0, 0] = fields_ref[0, 0] - time_step * (mach_number * sp + su + sz[nx:])
    out_ref[0, 1] = fields_ref[0, 1] - time_step * (mach_number * su + sp)
    out_ref[0, 2] = fields_ref[0, 2] - (time_step * mach_number) * sv
    out_ref[0, 3] = fields_ref[0, 3] - time_step * (mach_number * sw + sz[:nx])


def filter_kernel(fields_ref, fx_ref, fz_ref, out_ref):
    nz = fields_ref.shape[3]
    nx = fields_ref.shape[2]
    fx = split_parts(fx_ref[...])
    fzt = split_parts(fz_ref[...])
    sx = dot_parts(fx, split_parts(wide(fields_ref)))
    sz = dot_parts(split_parts(jnp.concatenate([fields_ref[0, i] for i in range(4)], axis=0)), fzt)
    for i in range(4):
        out_ref[0, i] = fields_ref[0, i] + filter_weight * (sx[:, i * nz:(i + 1) * nz] + sz[i * nx:(i + 1) * nx])


def row_call(kernel, fields, mat_x, mat_zt):
    rows, count, nx, nz = fields.shape
    block = pl.BlockSpec((1, count, nx, nz), lambda i: (i, 0, 0, 0))
    return pl.pallas_call(
        kernel,
        grid=(rows,),
        in_specs=[block, pl.BlockSpec((nx, nx), lambda i: (0, 0)), pl.BlockSpec((nz, nz), lambda i: (0, 0))],
        out_specs=block,
        out_shape=jax.ShapeDtypeStruct(fields.shape, jnp.float32),
        cost_estimate=pl.CostEstimate(
            flops=6 * rows * count * nx * nz * (nx + nz), bytes_accessed=8 * fields.size, transcendentals=0
        ),
    )(fields, mat_x, mat_zt)


def chain(streams, slabs):
    side = math.isqrt(streams)
    path = list(range(streams))
    if side * side == streams:
        path = [r * side + (c if r % 2 == 0 else side - 1 - c) for r in range(side) for c in range(side)]
    place = [path.index(s) for s in range(streams)]
    order = []
    for k in range(slabs):
        order += [s * slabs + k for s in (path if k % 2 == 0 else path[::-1])]
    return place, order


def neighbour_rows(values, width, order, sections):
    rows = values.shape[0]
    total = len(order)
    axes = ("section", "stream", "slab")

    def shift(part, steps):
        pairs = []
        for section in range(sections):
            for g in range(total):
                if 0 <= g + steps < total:
                    pairs.append((section * total + order[g], section * total + order[g + steps]))
        return lax.ppermute(part, axes, pairs)

    if rows >= width:
        return shift(values[rows - width:], 1), shift(values[:width], -1)
    reach = -(-width // rows)
    before = jnp.concatenate([shift(values, d) for d in range(reach, 0, -1)], axis=0)
    after = jnp.concatenate([shift(values, -d) for d in range(1, reach + 1)], axis=0)
    return before[reach * rows - width:], after[:width]


def slope(values, dim):
    pads = [(0, 0)] * values.ndim
    pads[dim] = (1, 1)
    padded = jnp.pad(values, pads)
    length = values.shape[dim]
    return 0.5 * (
        lax.slice_in_dim(padded, 2, length + 2, axis=dim) - lax.slice_in_dim(padded, 0, length, axis=dim)
    )


def lamb(fields, before, after):
    u, v, w = fields[:, 1], fields[:, 2], fields[:, 3]
    rows = fields.shape[0]
    near = jnp.concatenate([before, jnp.stack([u, w], axis=1), after], axis=0)
    c2 = 0.5 * (near[2:] - near[:rows])
    ox = c2[:, 1] - slope(v, 2)
    oy = slope(u, 2) - slope(w, 1)
    oz = slope(v, 1) - c2[:, 0]
    return jnp.stack([oy * w - oz * v, oz * u - ox * w, ox * v - oy * u], axis=1)


def shift_masked(value, dim, step):
    size = value.shape[dim]
    moved = pltpu.roll(value, (-step) % size, dim)
    index = lax.broadcasted_iota(jnp.int32, value.shape, dim)
    return jnp.where(index == (size - 1 if step > 0 else 0), 0.0, moved)


def inner_slope(value, dim):
    return 0.5 * (shift_masked(value, dim, 1) - shift_masked(value, dim, -1))


def fold(index, side):
    row = index // side
    col = index % side
    return row * side + col + (row % 2) * (side - 1 - 2 * col)


def steps_kernel(streams, slabs, cells_ref, region_ref, dx_ref, dz_ref, fx_ref, fz_ref, out_ref,
                 pv, uw, ghost, part, source, forcing, dxs, dzs, fxs, fzs, pv_send, pv_recv, give_send, uw_send, uw_recv, src_send, src_recv, row_send, row_recv,
                 in_send, in_recv, far_send, far_recv, credit, go, give_free, half_send, half_recv):
    _, span, _, width, nz = cells_ref.shape
    nx = width * streams
    rows = span // streams
    half = span // 2
    side = math.isqrt(streams)
    section, stream, slab = lax.axis_index("section"), lax.axis_index("stream"), lax.axis_index("slab")
    is_flow, is_sound = section == 0, section == 1
    count = rows + (1 - section) * (span - rows)
    pairs = SEGMENTS // 2

    def turn(place, which):
        return place + (which % 2) * (streams - 1 - 2 * place)

    def chunk_of(which):
        return turn(fold(which, side), slab)

    own = chunk_of(stream)
    base = own * rows

    def chain_step(step):
        place = own + step
        inside = (place >= 0) & (place < streams)
        peer = fold(turn(jnp.clip(place, 0, streams - 1), slab), side)
        sound = jnp.where(inside, peer, stream)
        level = jnp.where(inside & is_sound, slab, slab + step)
        valid = (level >= 0) & (level < slabs)
        return (section, jnp.where(is_flow, stream, sound), jnp.clip(level, 0, slabs - 1)), valid

    low, has_low = chain_step(-1)
    high, has_high = chain_step(1)
    partner = (1 - section, stream, slab)

    def remote(src, dst, send, recv, device):
        return pltpu.make_async_remote_copy(
            src_ref=src, dst_ref=dst, send_sem=send, recv_sem=recv,
            device_id=device, device_id_type=pl.DeviceIdType.MESH,
        )

    def axial(which):
        return pl.ds(pl.multiple_of(which * width, width), width)

    last = streams - 1
    at_start, at_end = own == 0, own == last
    takes = is_flow & ((at_end & has_high) | (at_start & has_low))
    edge_side = at_end.astype(jnp.int32)
    above_slab, below_slab = jnp.minimum(slab + 1, slabs - 1), jnp.maximum(slab - 1, 0)
    cut_chips = (
        (section, fold(turn(last, slab), side), above_slab),
        (section, fold(turn(0, slab), side), below_slab),
    )
    cut_level = jnp.where(at_end, high[2], low[2])
    cut_peer = (section, stream, cut_level)

    def pv_up(slot, deep, piece):
        cut = axial(piece)
        return remote(
            pv.at[slot, pl.ds(count - 2, 2), :, cut], ghost.at[deep, 0, :, :, cut],
            pv_send.at[deep, 0, piece], pv_recv.at[deep, 0, piece], high,
        )

    def pv_down(slot, deep, piece):
        cut = axial(piece)
        return remote(
            pv.at[slot, pl.ds(0, 2), :, cut], ghost.at[deep, 1, :, :, cut],
            pv_send.at[deep, 1, piece], pv_recv.at[deep, 1, piece], low,
        )

    has_side = (has_high, has_low)
    corner = streams - 1 - stream
    giving, helping = [], []
    for gap in range(2):
        target = cut_chips[gap][1]
        giving.append(is_flow & has_side[gap] & (stream != target) & (corner != target))
        helping.append(is_flow & has_side[gap] & (stream == target + 2 - 4 * (target // 2)))

    def giver(t):
        return (section, (stream + t) % streams, jnp.where(at_end, above_slab, below_slab))

    def half_of(piece, part):
        return pl.ds(pl.multiple_of(piece * width + part * (width // 2), width // 2), width // 2)

    def give(gap, slot, deep):
        cut = axial(stream)
        first = (count - 2, 0)[gap]
        return remote(
            pv.at[slot, pl.ds(first, 2), :, cut], ghost.at[deep, gap, :, :, cut],
            give_send.at[deep, gap, 0], pv_recv.at[deep, gap, stream], cut_chips[gap],
        )

    def give_half(gap, slot, deep, piece):
        cut = half_of(piece, 0)
        first = (count - 2, 0)[gap]
        return remote(
            pv.at[slot, pl.ds(first, 2), :, cut], ghost.at[deep, gap, :, :, cut],
            give_send.at[deep, gap, 1], pv_recv.at[deep, gap, piece], cut_chips[gap],
        )

    def cut_half(slot, deep):
        cut = half_of(corner, 1)
        return remote(
            pv.at[slot, pl.ds(edge_side * (count - 2), 2), :, cut], ghost.at[deep, 1 - edge_side, :, :, cut],
            half_send.at[deep], half_recv.at[deep], cut_peer,
        )

    def half_landing(deep, part):
        landed = ghost.at[deep, edge_side, :, :, half_of(corner, part)]
        semaphore = pv_recv.at[deep, edge_side, corner] if part == 0 else half_recv.at[deep]
        return remote(landed, landed, half_send.at[deep], semaphore, cut_peer)

    def uw_copy():
        return remote(
            uw.at[jnp.where(at_start, 1, span)], uw.at[jnp.where(at_start, span + 1, 0)], uw_send, uw_recv, cut_peer
        )

    def uw_landing():
        landed = uw.at[jnp.where(at_start, 0, span + 1)]
        return remote(landed, landed, uw_send, uw_recv, cut_peer)

    def src_copy(slot):
        return remote(source, forcing.at[slot], src_send.at[slot], src_recv.at[slot], partner)

    def sends_high(piece):
        return has_high & (is_sound | jnp.logical_not(at_end) | (piece == stream))

    def sends_low(piece):
        return has_low & (is_sound | jnp.logical_not(at_start) | (piece == stream))

    def start_piece(slot, deep, piece):
        for gap in range(2):
            pl.when(giving[gap] & (piece == stream))(lambda: give(gap, slot, deep).start())
            pl.when(helping[gap] & (piece == streams - 1 - cut_chips[gap][1]))(
                lambda: give_half(gap, slot, deep, piece).start()
            )
        pl.when(takes & (piece == corner))(lambda: cut_half(slot, deep).start())

        @pl.when(sends_high(piece))
        def _():
            pv_up(slot, deep, piece).start()

        @pl.when(sends_low(piece))
        def _():
            pv_down(slot, deep, piece).start()

    def wait_piece(slot, deep, piece):
        split = takes & (piece == corner)

        @pl.when(has_low & jnp.logical_not(split & at_start))
        def _():
            pv_up(slot, deep, piece).wait_recv()

        @pl.when(has_high & jnp.logical_not(split & at_end))
        def _():
            pv_down(slot, deep, piece).wait_recv()

        @pl.when(split)
        def _():
            half_landing(deep, 0).wait_recv()
            half_landing(deep, 1).wait_recv()

        for gap in range(2):
            pl.when(giving[gap] & (piece == stream))(lambda: give(gap, slot, deep).wait_send())
            pl.when(helping[gap] & (piece == streams - 1 - cut_chips[gap][1]))(
                lambda: give_half(gap, slot, deep, piece).wait_send()
            )
        pl.when(takes & (piece == corner))(lambda: cut_half(slot, deep).wait_send())

        @pl.when(sends_high(piece))
        def _():
            pv_up(slot, deep, piece).wait_send()

        @pl.when(sends_low(piece))
        def _():
            pv_down(slot, deep, piece).wait_send()

    def repeat(start, stop, body):
        def step(i, carry):
            body(i)
            return carry

        lax.fori_loop(start, stop, step, 0)

    barrier = pltpu.get_barrier_semaphore()

    def greet(device):
        pl.semaphore_signal(barrier, inc=1, device_id=device, device_id_type=pl.DeviceIdType.MESH)

    greet(partner)
    for t in range(1, streams):
        greet((section, (stream + t) % streams, slab))

    @pl.when(slab > 0)
    def _():
        greet((section, stream, slab - 1))

    @pl.when(slab < slabs - 1)
    def _():
        greet((section, stream, slab + 1))

    for gap in range(2):
        pl.when(giving[gap])(lambda: greet(cut_chips[gap]))

    @pl.when(takes)
    def _():
        for t in range(1, streams):
            pl.when((stream + t) % streams != corner)(lambda: greet(giver(t)))

    around = [slab > 0, slab < slabs - 1, giving[0], giving[1]] + [takes] * (streams - 2)
    pl.semaphore_wait(barrier, streams + sum(flag.astype(jnp.int32) for flag in around))

    def held(kind, which, first, lines):
        target = (pv.at[0, pl.ds(first, lines)], uw.at[pl.ds(1 + first, lines)])[kind]
        return target.at[:, :, axial(which)]

    def landing(kind, which, first, lines, recv, sender):
        landed = held(kind, which, first, lines)
        return remote(landed, landed, recv, recv, (section, sender, slab))

    beside = (stream + 1 - 2 * (stream % 2), stream + 2 - 4 * (stream // 2))
    across = streams - 1 - stream

    def near_copy(kind, j):
        return remote(
            cells_ref.at[kind], held(kind, stream, 0, span),
            in_send.at[kind, j], in_recv.at[kind, j], (section, beside[j], slab),
        )

    def far_copy(kind, j):
        passed = held(kind, beside[j], j * half, half)
        return remote(passed, passed, far_send.at[kind, j], far_recv.at[kind, j], (section, beside[1 - j], slab))

    def clear_ends():
        zero = jnp.zeros((2, nx, nz), jnp.float32)

        @pl.when(jnp.logical_not(has_low))
        def _():
            for deep in range(4):
                for line in range(2):
                    ghost[deep, 0, line] = zero
            uw[0] = zero

        @pl.when(jnp.logical_not(has_high))
        def _():
            for deep in range(4):
                for line in range(2):
                    ghost[deep, 1, line] = zero
            uw[count + 1] = zero

    def split_matrices():
        clear_ends()
        dxs[0], dxs[1] = split_parts(time_step * mach_number * dx_ref[...])
        fxs[0], fxs[1] = split_parts(filter_weight * fx_ref[...])
        for target, matrix in ((dzs, time_step * dz_ref[...].T), (fzs, filter_weight * fz_ref[...].T)):
            high_part, low_part = split_parts(matrix)
            target[...] = jnp.concatenate(
                [
                    jnp.concatenate([high_part, low_part], axis=1),
                    jnp.concatenate([high_part, jnp.zeros_like(low_part)], axis=1),
                ],
                axis=0,
            )

    @pl.when(is_flow)
    def _():
        for kind in range(2):
            for j in range(2):
                near_copy(kind, j).start()
        pv[0, 0:span, :, axial(stream)] = cells_ref[0]
        uw[1:span + 1, :, axial(stream)] = cells_ref[1]
        start_piece(0, 0, stream)
        split_matrices()
        for kind in range(2):
            for j in range(2):
                landing(kind, beside[j], 0, span, in_recv.at[kind, j], beside[j]).wait_recv()
                far_copy(kind, j).start()
                if kind == 0:
                    start_piece(0, 0, beside[j])
        for kind in range(2):
            for j in range(2):
                landing(kind, across, j * half, half, far_recv.at[kind, j], beside[1 - j]).wait_recv()
            if kind == 0:
                start_piece(0, 0, across)
        pl.when(takes)(lambda: uw_copy().start())
        pl.semaphore_signal(go, inc=1, device_id=partner, device_id_type=pl.DeviceIdType.MESH)
        for kind in range(2):
            for j in range(2):
                near_copy(kind, j).wait_send()
                far_copy(kind, j).wait_send()

    def in_copy(kind, t):
        peer = (stream + t) % streams
        return remote(
            cells_ref.at[kind, pl.ds(chunk_of(peer) * rows, rows)], held(kind, stream, 0, rows),
            in_send.at[kind, t - 1], in_recv.at[kind, t - 1], (section, peer, slab),
        )

    @pl.when(is_sound)
    def _():
        split_matrices()
        pv[0, 0:rows, :, axial(stream)] = cells_ref[0, pl.ds(base, rows)]
        uw[1:rows + 1, :, axial(stream)] = cells_ref[1, pl.ds(base, rows)]
        pl.semaphore_wait(go, 1)
        for kind in range(2):
            for t in range(1, streams):
                in_copy(kind, t).start()
        start_piece(0, 0, stream)
        for kind in range(2):
            for t in range(1, streams):
                sender = (stream + streams - t) % streams
                in_copy(kind, t).wait_send()
                landing(kind, sender, 0, rows, in_recv.at[kind, t - 1], sender).wait_recv()
                if kind == 0:
                    start_piece(0, 0, sender)

    def along_x(mats, fields):
        upper = jnp.concatenate([h for h, l in fields], axis=1)
        lower = jnp.concatenate([l for h, l in fields], axis=1)
        result = dot_parts(mats, (upper, lower))
        return [result[:, i * nz:(i + 1) * nz] for i in range(len(fields))]

    def along_z(mats, fields):
        stacked = jnp.concatenate([jnp.concatenate(field, axis=1) for field in fields], axis=0)
        result = jnp.dot(stacked, mats, preferred_element_type=jnp.float32)
        result = result[:, :nz] + result[:, nz:]
        size = result.shape[0] // len(fields)
        return [result[i * size:(i + 1) * size] for i in range(len(fields))]

    def advance(slot, row, inner):
        p, v, u, w = pv[slot, row, 0], pv[slot, row, 1], uw[row + 1, 0], uw[row + 1, 1]
        fields = [split_parts(field) for field in (p, u, v, w)]
        sp, su, sv, sw = along_x((dxs[0], dxs[1]), fields)
        zp, zw = along_z(dzs[...], (fields[0], fields[3]))
        new_p = p - sp - (su + su) - zw
        new_v = v - sv
        if inner:
            def slope_y(field):
                ahead = pv[slot, row + 1, field] - pv[slot, row - 1, field]
                return near_weight * ahead - far_weight * (pv[slot, row + 2, field] - pv[slot, row - 2, field])

            new_p = new_p - slope_y(1)
            new_v = new_v - slope_y(0)
        pv[1 - slot, row, 0] = new_p
        pv[1 - slot, row, 1] = new_v
        uw[row + 1, 0] = u - su - (sp + sp)
        uw[row + 1, 1] = w - sw - zp

    def advance_two(slot, row, inner):
        advance(slot, row, inner)
        advance(slot, row + 1, inner)

    def rim_rows(slot):
        advance_two(slot, 0, False)
        advance_two(slot, count - 2, False)

    def inner_rows(slot, start, stop):
        limit = count // 2 - 1
        repeat(jnp.minimum(1 + start, limit), jnp.minimum(1 + stop, limit), lambda k: advance_two(slot, 2 * k, True))

    def add_forcing(slot, held_in):
        def body(row):
            uw[row + 1, 0] = uw[row + 1, 0] + time_step * forcing[held_in, row, 0]
            pv[1 - slot, row, 1] = pv[1 - slot, row, 1] + time_step * forcing[held_in, row, 1]
            uw[row + 1, 1] = uw[row + 1, 1] + time_step * forcing[held_in, row, 2]

        repeat(0, rows, body)

    def finish_rim(slot, deep, early, send, late):
        for gap in range(2):
            pl.when(giving[gap] & late & send)(lambda: pl.semaphore_wait(give_free.at[gap], 1))

        def one(piece):
            cut = axial(piece)
            wait_piece(slot, deep, piece)

            for field in range(2):
                def line(row):
                    return pv[slot, row, field, cut]

                def below(which):
                    return ghost[deep, 0, which, field, cut]

                def above(which):
                    return ghost[deep, 1, which, field, cut]

                def change(row, near, far):
                    spot = pv.at[1 - slot, row, 1 - field, cut]
                    spot[...] = spot[...] - (near_weight * near - far_weight * far)

                change(0, line(1) - below(1), line(2) - below(0))
                change(1, line(2) - line(0), line(3) - below(1))
                change(count - 2, line(count - 1) - line(count - 3), above(0) - line(count - 4))
                change(count - 1, above(0) - line(count - 2), above(1) - line(count - 3))

            @pl.when(send)
            def _():
                start_piece(1 - slot, (deep + 1) % 4, piece)

        done = 0
        for piece in range(streams):
            goal = (span // 2 - 2) * (piece + 1) // streams
            inner_rows(slot, done, goal)
            done = goal
            one(piece)
        @pl.when(takes & send)
        def _():
            advance_edge(deep)

        @pl.when(takes & early)
        def _():
            for t in range(1, streams):
                @pl.when((stream + t) % streams != corner)
                def _():
                    pl.semaphore_signal(
                        give_free.at[edge_side], inc=1, device_id=giver(t), device_id_type=pl.DeviceIdType.MESH
                    )

    def advance_edge(deep):
        row = jnp.where(at_start, 0, span + 1)
        p, u, w = ghost[deep, edge_side, 1 - edge_side, 0], uw[row, 0], uw[row, 1]
        fields = [split_parts(field) for field in (p, u, w)]
        sp, su, sw = along_x((dxs[0], dxs[1]), fields)
        uw[row, 0] = u - su - (sp + sp)
        uw[row, 1] = w - sw - along_z(dzs[...], (fields[0],))[0]

    def lamb_rows():
        def body(line):
            row = base + line
            u, v, w = uw[row + 1, 0], pv[0, row, 1], uw[row + 1, 1]
            ox = 0.5 * (uw[row + 2, 1] - uw[row, 1]) - inner_slope(v, 1)
            oy = inner_slope(u, 1) - inner_slope(w, 0)
            oz = inner_slope(v, 0) - 0.5 * (uw[row + 2, 0] - uw[row, 0])
            mask = -region_ref[line]
            source[line, 0] = mask * (oy * w - oz * v)
            source[line, 1] = mask * (oz * u - ox * w)
            source[line, 2] = mask * (ox * v - oy * u)

        def two(k):
            body(2 * k)
            body(2 * k + 1)

        repeat(0, rows // 2, two)

    def smooth(kind):
        def body(row):
            group = ((pv[0, row, 0], pv[0, row, 1]), (uw[row + 1, 0], uw[row + 1, 1]))[kind]
            fields = [split_parts(field) for field in group]
            sx = along_x((fxs[0], fxs[1]), fields)
            sz = along_z(fzs[...], fields)
            for i in range(2):
                part[kind, row, i] = group[i] + (sx[i] + sz[i])
            for t in range(1, streams):
                row_copy(kind, t, row).start()
            out_ref[kind, base + row] = part[kind, row, :, axial(stream)]

        repeat(0, rows, body)

    def smooth_own():
        mine = axial(stream)

        def body(row):
            group = (pv[0, row, 0], pv[0, row, 1], uw[row + 1, 0], uw[row + 1, 1])
            here = [pv[0, row, 0, mine], pv[0, row, 1, mine], uw[row + 1, 0, mine], uw[row + 1, 1, mine]]
            sx = along_x((fxs[0, mine], fxs[1, mine]), [split_parts(field) for field in group])
            sz = along_z(fzs[...], [split_parts(field) for field in here])
            for i in range(4):
                out_ref[i // 2, row, i % 2] = here[i] + (sx[i] + sz[i])

        repeat(0, span, body)

    def row_copy(kind, t, row):
        peer = (stream + t) % streams
        return remote(
            part.at[kind, row, :, axial(peer)], out_ref.at[kind, base + row],
            row_send.at[kind, t - 1, row], row_recv.at[kind, t - 1, row], (section, peer, slab),
        )

    def pair(m):
        more = m < pairs - 1
        which = m % 2
        deep = 2 * which

        @pl.when(is_flow)
        def _():
            @pl.when(takes & (m == 0))
            def _():
                uw_copy().wait_send()
                uw_landing().wait_recv()

            @pl.when(m > 0)
            def _():
                src_copy(1 - which).wait_send()

            lamb_rows()

            @pl.when(m > 1)
            def _():
                pl.semaphore_wait(credit, 1)

            src_copy(which).start()

        rim_rows(0)

        @pl.when(is_sound)
        def _():
            src_copy(which).wait_recv()
            add_forcing(0, which)

        finish_rim(0, deep, m < pairs - 2, True, m > 1)
        rim_rows(1)


        @pl.when(is_sound)
        def _():
            add_forcing(1, which)

            @pl.when(m < pairs - 2)
            def _():
                pl.semaphore_signal(credit, inc=1, device_id=partner, device_id_type=pl.DeviceIdType.MESH)

            @pl.when(m == pairs - 1)
            def _():
                smooth(1)

        finish_rim(1, deep + 1, m < pairs - 2, more, m > 0)
    repeat(0, pairs, pair)

    @pl.when(is_flow)
    def _():
        src_copy((pairs - 1) % 2).wait_send()
        smooth_own()

    @pl.when(is_sound)
    def _():
        smooth(0)

        for kind in (1, 0):
            def body(row):
                for t in range(1, streams):
                    sender = (stream + streams - t) % streams
                    landed = out_ref.at[kind, chunk_of(sender) * rows + row]
                    row_copy(kind, t, row).wait_send()
                    remote(
                        landed, landed, row_send.at[kind, t - 1, row], row_recv.at[kind, t - 1, row], (section, sender, slab)
                    ).wait_recv()

            repeat(0, rows, body)


def steps_call(streams, slabs, cells, region, deriv_x, deriv_z, filter_x, filter_z):
    _, span, _, width, nz = cells.shape
    nx = width * streams
    rows = span // streams
    f32 = jnp.float32
    dma = pltpu.SemaphoreType.DMA
    return pl.pallas_call(
        functools.partial(steps_kernel, streams, slabs),
        out_shape=jax.ShapeDtypeStruct(cells.shape, f32),
        in_specs=[pl.BlockSpec(memory_space=pltpu.VMEM)] * 6,
        out_specs=pl.BlockSpec(memory_space=pltpu.VMEM),
        scratch_shapes=[
            pltpu.VMEM((2, span, 2, nx, nz), f32),
            pltpu.VMEM((span + 2, 2, nx, nz), f32),
            pltpu.VMEM((4, 2, 2, 2, nx, nz), f32),
            pltpu.VMEM((2, rows, 2, nx, nz), f32),
            pltpu.VMEM((rows, 3, nx, nz), f32),
            pltpu.VMEM((2, rows, 3, nx, nz), f32),
            pltpu.VMEM((2, nx, nx), jnp.bfloat16),
            pltpu.VMEM((2 * nz, 2 * nz), jnp.bfloat16),
            pltpu.VMEM((2, nx, nx), jnp.bfloat16),
            pltpu.VMEM((2 * nz, 2 * nz), jnp.bfloat16),
            dma((4, 2, streams)), dma((4, 2, streams)), dma((4, 2, 2)), dma, dma, dma((2,)), dma((2,)),
            dma((2, streams - 1, rows)), dma((2, streams - 1, rows)), dma((2, streams - 1)), dma((2, streams - 1)),
            dma((2, 2)), dma((2, 2)),
            pltpu.SemaphoreType.REGULAR, pltpu.SemaphoreType.REGULAR, pltpu.SemaphoreType.REGULAR((2,)), dma((4,)), dma((4,)),
        ],
        compiler_params=pltpu.CompilerParams(
            collective_id=0, has_side_effects=True, vmem_limit_bytes=48 * 1024 * 1024
        ),
    )(cells, jnp.broadcast_to(region, (rows, nx, nz)), deriv_x, deriv_z, filter_x, filter_z)


def plain_steps(order, fields, region, deriv_x, deriv_zt, filter_x, filter_zt):
    rows = fields.shape[0]
    forcing = None
    for segment in range(SEGMENTS):
        pv = jnp.stack([fields[:, 0], fields[:, 2]], axis=1)
        before, after = neighbour_rows(pv, 2, order, 2)
        if segment % 2 == 0:
            uw = jnp.stack([fields[:, 1], fields[:, 3]], axis=1)
            low, high = neighbour_rows(uw, 1, order, 1)
            source = -region * lamb(fields, low, high)
            forcing = lax.ppermute(source, "section", [(0, 1)])
        part = row_call(local_kernel, fields, deriv_x, deriv_zt)
        near = jnp.concatenate([before, pv, after], axis=0)
        dy = (8.0 * (near[3:3 + rows] - near[1:1 + rows]) - (near[4:4 + rows] - near[:rows])) / 12.0
        fields = jnp.stack(
            [
                part[:, 0] - time_step * dy[:, 1],
                part[:, 1] + time_step * forcing[:, 0],
                part[:, 2] + time_step * (forcing[:, 1] - dy[:, 0]),
                part[:, 3] + time_step * forcing[:, 2],
            ],
            axis=1,
        )
    return row_call(filter_kernel, fields, filter_x, filter_zt)


def shards(state, source_mask, deriv_x, deriv_z, filter_x, filter_z):
    streams, slabs = lax.axis_size("stream"), lax.axis_size("slab")
    place, order = chain(streams, slabs)
    fields = state[0]
    count, width_x, width_y, nz = fields.shape
    nx = width_x * streams
    rows = width_y // streams
    even = lax.axis_index("slab") % 2 == 0
    back = [streams - 1 - p for p in place]

    blocks = source_mask.astype(jnp.float32)
    region = jnp.repeat(jnp.repeat(blocks, MBLK, axis=0), MBLK, axis=1).T
    mine = jnp.asarray(place)[lax.axis_index("stream")]
    mine = jnp.where(even, mine, streams - 1 - mine)
    region = lax.dynamic_slice_in_dim(region, mine * rows, rows, 0)[:, None, :, None]
    deriv_zt, filter_zt = deriv_z.T, filter_z.T

    mats = (deriv_x, deriv_zt, filter_x, filter_zt)
    if rows >= 4 and streams == 4:
        cells = fields.reshape(count // 2, 2, width_x, width_y, nz).transpose(1, 3, 0, 2, 4)
        cells = steps_call(streams, slabs, cells, region[:, 0], deriv_x, deriv_z, filter_x, filter_z)
        return cells.transpose(2, 0, 3, 1, 4).reshape(1, count, width_x, width_y, nz)
    parts = fields.reshape(count, width_x, streams, rows, nz).transpose(2, 3, 0, 1, 4)
    parts = jnp.where(even, jnp.stack([parts[p] for p in place]), jnp.stack([parts[p] for p in back]))
    parts = lax.all_to_all(parts, "stream", split_axis=0, concat_axis=0, tiled=True)
    fields = parts.transpose(1, 2, 0, 3, 4).reshape(rows, count, nx, nz)
    fields = plain_steps(order, fields, region, *mats)

    parts = fields.reshape(rows, count, streams, width_x, nz).transpose(2, 0, 1, 3, 4)
    parts = lax.all_to_all(parts, "stream", split_axis=0, concat_axis=0, tiled=True)
    inv_place = [place.index(j) for j in range(streams)]
    inv_back = [back.index(j) for j in range(streams)]
    parts = jnp.where(even, jnp.stack([parts[p] for p in inv_place]), jnp.stack([parts[p] for p in inv_back]))
    return parts.transpose(2, 3, 0, 1, 4).reshape(1, count, width_x, width_y, nz)


def solution(mesh):
    placed = (P("section", None, "stream", "slab", None), P(None, "slab"), P(), P(), P(), P())
    return jax.shard_map(
        shards,
        mesh=mesh,
        in_specs=placed,
        out_specs=P("section", None, "stream", "slab", None),
        check_vma=False,
    )
```
